32 devices in a mesh: groups: 2 (over y), exp: 4 (over z), patch: 2 (over x), band: 2 (over core).
Axes of the slice: x: 2, y: 2, z: 4, core: 2. Of those that a mesh axis runs over, the one named last changes fastest.
Arguments:
- templates: bfloat16 [8, 8, 256, 256], P(('groups', 'exp'), 'patch', None, 'band'), parts along dimension 0, may hold values from -6 to 6
- exposures: bfloat16 [8, 4, 4, 256, 256], P(('groups', 'exp'), 'patch', None, None, 'band'), parts along dimension 0, may hold values from -6 to 6
- variance: float32 [8, 4, 4, 256, 256], P(('groups', 'exp'), 'patch', None, None, 'band'), parts along dimension 0, may hold values from 0.5 to 4
- coefficients: float32 [8, 4, 4, 27], P(('groups', 'exp'), 'patch'), parts along dimension 0, may hold values from -1.2 to 1.2
- psf_width: float32 [8, 4, 4, 2], P(('groups', 'exp'), 'patch'), parts along dimension 0, may hold values from 1 to 2.5
- patch_ids: int32 [8, 4, 4], P(('groups', 'exp'), 'patch'), parts along dimension 0, may hold values from 0 to 23
- live_count: int32 [8, 4], P(('groups', 'exp'), 'patch'), parts along dimension 0, may hold values from 1 to 4
Outputs:
- coadd_diff: float32 [8, 8, 256, 256], P(('groups', 'exp'), 'patch', None, 'band'), parts along dimension 0
- score: float32 [8, 4, 4, 256, 256], P(('groups', 'exp'), 'patch', None, None, 'band'), parts along dimension 0
The draws below stay inside these ranges and needn't reach their ends.
There are 2 independent parts, one for each index of `groups`. The reference program is written for one: setup_inputs(seed, part) draws one part's arguments, and reference() takes and returns one part's arrays. A program takes and returns all parts, laid end to end along the dimension named above; each array names one. Nothing has to cross between parts.
Inputs may be any that keep to these rules, and one draw needn't show every extreme that they name: `patch_ids`: an id names patch id % 8 of the grid row id // 8 - 1 relative to the exposure's own row. `live_count`: sub-tiles at slots below the count are live.
All inputs are finite; a program needn't handle non-finite values.
Results may differ from the reference program's by a relative error of at most 0.0049.
Values may be sent and summed in bfloat16 or wider, within the bound.
No kernel may reach another device: no remote copies, remote signals or barrier semaphores. Data moves between devices by JAX's collectives and lax.ppermute only.
A program may use at most 64 MiB of HBM per device.

```python
import math
import jax
import jax.numpy as jnp
import numpy as np
from jax import lax

S = 256
K = 4
NB = 27
HW = 10
PW = 7
NX = 4
NP = 8
NE = 4


def set_ends(entries, own_key, least, high):
    spot = [jax.random.randint(jax.random.fold_in(own_key, axis), (), 0, length) for axis, length in enumerate(entries.shape)]
    main_axis = entries.shape.index(max(entries.shape))
    neighbour = spot[:main_axis] + [(spot[main_axis] + 1) % entries.shape[main_axis]] + spot[main_axis + 1:]
    return entries.at[tuple(spot)].set(least).at[tuple(neighbour)].set(high)


def steps_of(stream_key, dims, shards, smallest, high):
    factor_of = 1.0
    for position, shards_of in shards:
        draws = jax.random.uniform(jax.random.fold_in(jax.random.fold_in(stream_key, 6), position), (shards_of,), jnp.float32, smallest / len(shards), high / len(shards))
        factor_of = factor_of * jnp.repeat(jnp.exp(draws), dims[position] // shards_of).reshape((-1,) + (1,) * (len(dims) - 1 - position))
    return factor_of


def bell_draw(own_key, extent, scale, most, pieces=(), kind=jnp.bfloat16):
    level = steps_of(own_key, extent, pieces, -0.22, 0.18) if pieces else 1.0
    values = jax.random.normal(own_key, extent, jnp.float32) * scale * level
    return jnp.minimum(jnp.maximum(values, -most), most).astype(kind)


def setup_inputs(seed: int = 0, part: int = 0) -> dict:
    streams_of = jax.random.split(jax.random.key(seed), 8)
    part_keys = jax.random.split(jax.random.fold_in(streams_of[7], part), 8)
    templates = bell_draw(part_keys[0], (NX, NP, S, S), 1.0, 6.0, ((0, 4), (1, 2), (3, 2)))
    exposures = bell_draw(part_keys[1], (NX, NE, K, S, S), 1.0, 6.0, ((0, 4), (1, 2), (4, 2)))
    variance = jnp.clip(jnp.exp(math.log(4.0) - 2.0794415 * jax.random.uniform(part_keys[2], (NX, NE, K, S, S), jnp.float32) ** steps_of(part_keys[2], (NX, NE, K, S, S), ((0, 4), (1, 2), (4, 2)), -0.2, 0.2)), 0.5, 4.0)
    coefficients = bell_draw(part_keys[3], (NX, NE, K, NB), 0.2, 1.2, ((0, 4), (1, 2)), jnp.float32)
    psf_width = jnp.clip(jnp.exp(math.log(2.5) - 0.916290732 * jax.random.uniform(part_keys[4], (NX, NE, K, 2), jnp.float32) ** steps_of(part_keys[4], (NX, NE, K, 2), ((0, 4), (1, 2)), -0.2, 0.2)), 1.0, 2.5)
    patch_ids = set_ends(jax.random.randint(part_keys[5], (NX, NE, K), 0, 3 * NP), jax.random.fold_in(part_keys[5], 1), 0, (3 * NP) - 1).astype(jnp.int32)
    live_count = set_ends(jax.random.randint(part_keys[6], (NX, NE), 1, K + 1), jax.random.fold_in(part_keys[6], 1), 1, K).astype(jnp.int32)
    return dict(templates=templates, exposures=exposures, variance=variance, coefficients=coefficients, psf_width=psf_width, patch_ids=patch_ids, live_count=live_count)


sigmas = (0.75, 1.5, 3.0)
degrees = (4, 2, 2)

def basis_terms():
    terms = []
    offset = 0
    for group in range(3):
        for first in range(degrees[group] + 1):
            for second in range(degrees[group] + 1 - first):
                terms.append((group, first, second, offset + first))
        offset = offset + degrees[group] + 1
    return terms

def membership():
    table = np.zeros((27, 11), np.float32)
    for index, term in enumerate(basis_terms()):
        table[index, term[3]] = 1.0
    return table

def profile(offset, sigma, power, reach):
    grid = jnp.arange(-reach, reach + 1).astype(jnp.float32)
    base = jnp.exp(-grid * grid / (2.0 * sigma * sigma)) * (grid / reach) ** power
    scale = jnp.sqrt(jnp.sum(base * base))
    spot = offset.astype(jnp.float32)
    value = jnp.exp(-spot * spot / (2.0 * sigma * sigma)) * (spot / reach) ** power / scale
    return jnp.where(jnp.abs(offset) <= reach, value, jnp.zeros_like(value))

def row_tables(count, reach):
    index = jnp.arange(count, dtype=jnp.int32)
    offset = index[:, None] - index[None, :]
    tables = []
    for group in range(3):
        for first in range(degrees[group] + 1):
            tables.append(profile(offset, sigmas[group], first, reach))
    return jnp.stack(tables).astype(jnp.bfloat16)

def column_tables(cols_in, cols_out, shift, reach):
    inner = jnp.arange(cols_in, dtype=jnp.int32)[:, None]
    outer = jnp.arange(cols_out, dtype=jnp.int32)[None, :]
    offset = outer + shift - inner
    return jnp.stack([profile(offset, sigmas[term[0]], term[2], reach) for term in basis_terms()])

def psf_table(offset, width, reach):
    grid = jnp.arange(-reach, reach + 1).astype(jnp.float32)
    total = jnp.sum(jnp.exp(-grid * grid / (2.0 * width * width)))
    spot = offset.astype(jnp.float32)
    value = jnp.exp(-spot * spot / (2.0 * width * width)) / total
    return jnp.where(jnp.abs(offset) <= reach, value, jnp.zeros_like(value))

def reference(templates, exposures, variance, coefficients, psf_width, patch_ids, live_count):
    padded = jnp.pad(templates, ((1, 1), (0, 0), (0, 0), (0, 0)))
    grid_row = jnp.arange(NX, dtype=jnp.int32)[:, None, None] + patch_ids // NP
    grid_col = patch_ids % NP
    live = (jnp.arange(K, dtype=jnp.int32)[None, None, :] < live_count[:, :, None]).astype(jnp.float32)
    chosen = padded[grid_row, grid_col].reshape(-1, S, S)
    gr_flat = row_tables(S, HW).reshape(-1, S)
    col_tab = column_tables(S, S, 0, HW)
    member = jnp.asarray(membership())
    index = jnp.arange(S, dtype=jnp.int32)
    offset_rows = index[:, None] - index[None, :]
    offset_cols = index[None, :] - index[:, None]

    def slot_work(items):
        template, exposure, var_tile, coeff, width, alive = items
        rows = jnp.dot(gr_flat, template, preferred_element_type=jnp.float32).astype(jnp.bfloat16).reshape(11, S, S)
        mixing = coeff[:, None] * member
        mats = jnp.einsum('kp,kcd->pcd', mixing, col_tab, precision=lax.Precision.HIGHEST).astype(jnp.bfloat16)
        convolved = jnp.einsum('psc,pcd->sd', rows.astype(jnp.float32), mats.astype(jnp.float32))
        weight = 1.0 / var_tile
        weighted = (exposure.astype(jnp.float32) - convolved) * weight
        prow = psf_table(offset_rows, width[0], PW)
        pcol = psf_table(offset_cols, width[1], PW)
        numer = jnp.dot(prow.astype(jnp.bfloat16), weighted.astype(jnp.bfloat16), preferred_element_type=jnp.float32).astype(jnp.bfloat16)
        numer = jnp.dot(numer, pcol.astype(jnp.bfloat16), preferred_element_type=jnp.float32)
        denom = jnp.dot((prow * prow).astype(jnp.bfloat16), weight.astype(jnp.bfloat16), preferred_element_type=jnp.float32).astype(jnp.bfloat16)
        denom = jnp.dot(denom, (pcol * pcol).astype(jnp.bfloat16), preferred_element_type=jnp.float32)
        return (alive * numer / jnp.sqrt(denom), alive * weighted)
    score, masked = lax.map(slot_work, (chosen, exposures.reshape(-1, S, S), variance.reshape(-1, S, S), coefficients.reshape(-1, NB), psf_width.reshape(-1, 2), live.reshape(-1)))
    coadd = jnp.zeros((NX + 2, NP, S, S), jnp.float32).at[grid_row.reshape(-1), grid_col.reshape(-1)].add(masked)
    return (coadd[1:-1], score.reshape(NX, NE, K, S, S))
```

```python
import functools

import jax
import jax.numpy as jnp
import numpy as np
from jax import lax
from jax.experimental import pallas as pl
from jax.experimental.pallas import tpu as pltpu
from jax.sharding import PartitionSpec as P

HW = 10
PW = 7

sigmas = (0.75, 1.5, 3.0)
degrees = (4, 2, 2)

VMEM = pltpu.VMEM
SMEM = pltpu.SMEM


def shifted(block, axis, distance):
    devices = range(lax.axis_size(axis))
    route = [(i - distance, i) for i in devices if i - distance in devices]
    return lax.ppermute(block, axis, route)


def fetched(block, axis, distance):
    devices = lax.axis_size(axis)
    return lax.ppermute(block, axis, [((i + distance) % devices, i) for i in range(devices)])


def sent(block, axis, distance):
    devices = lax.axis_size(axis)
    return lax.ppermute(block, axis, [(i, (i + distance) % devices) for i in range(devices)])


def basis_terms():
    terms = []
    offset = 0
    for group in range(3):
        for first in range(degrees[group] + 1):
            for second in range(degrees[group] + 1 - first):
                terms.append((group, first, second, offset + first))
        offset = offset + degrees[group] + 1
    return terms


def profile(offset, sigma, power, reach):
    grid = np.arange(-reach, reach + 1).astype(np.float32)
    base = np.exp(-grid * grid / np.float32(2.0 * sigma * sigma)) * (grid / reach) ** power
    scale = np.sqrt(np.sum(base * base))
    spot = offset.astype(np.float32)
    value = np.exp(-spot * spot / np.float32(2.0 * sigma * sigma)) * (spot / reach) ** power / scale
    return np.where(np.abs(offset) <= reach, value, 0.0).astype(np.float32)


def row_tables(count, reach):
    index = np.arange(count)
    offset = index[:, None] - index[None, :]
    tables = []
    for group in range(3):
        for first in range(degrees[group] + 1):
            tables.append(profile(offset, sigmas[group], first, reach))
    return np.stack(tables)


def ring_offset(width):
    lane = np.arange(width)
    return np.where(lane < width // 2, lane, lane - width)


def ring_profiles(width, reach):
    offset = ring_offset(width)
    return np.stack([profile(offset, sigmas[t[0]], t[2], reach) for t in basis_terms()])


def prepare_kernel(width_ref, live_ref, core_ref, coeff_ref, ring_ref, own_ref, other_ref,
                   norm_ref, inv_ref, prow_ref, pcol_ref, mats_ref, dist_ref, near_ref):
    tiles, size, cols = own_ref.shape
    wide = 2 * cols
    rows = lax.broadcasted_iota(jnp.int32, (size, size), 0)
    across = lax.broadcasted_iota(jnp.int32, (size, size), 1)
    gap = rows - across
    dist_ref[...] = (gap * gap).astype(jnp.float32)
    inner = lax.broadcasted_iota(jnp.int32, (wide, wide), 0)
    outer = lax.broadcasted_iota(jnp.int32, (wide, wide), 1)
    ring = jnp.abs(inner - outer)
    ring = jnp.minimum(ring, wide - ring)
    near_ref[...] = (ring * ring).astype(jnp.float32)
    lane = lax.broadcasted_iota(jnp.int32, (size, cols), 1)
    half = cols // 2
    keep = (lane >= half) == (core_ref[0] == 1)
    limit = float(PW * PW)
    spot = lax.broadcasted_iota(jnp.int32, (8, 128), 1)
    spot_low = spot.astype(jnp.float32) - PW

    terms = basis_terms()
    profiles = max(t[3] for t in terms) + 1

    def scale_of(width):
        rate = -0.5 / (width * width)
        base = jnp.where(spot <= 2 * PW, jnp.exp(spot_low * spot_low * rate), 0.0)
        return rate, 1.0 / jnp.sum(base[0:1], axis=1, keepdims=True)

    def one(t, carry):
        inv_own = 1.0 / own_ref[t]
        inv_other = jnp.where(keep, 1.0 / other_ref[t], 0.0)
        inv_ref[t, :, :cols] = inv_own
        inv_ref[t, :, cols:] = inv_other
        inv_low = jnp.concatenate([inv_own, inv_other], axis=1).astype(jnp.bfloat16)
        rate, scale = scale_of(jnp.full((8, 128), width_ref[t, 0], jnp.float32))
        rate = rate[0:1, 0:1]
        dist = dist_ref[...]
        prow = jnp.where(dist <= limit, jnp.exp(dist * rate) * scale, 0.0)
        prow_ref[t] = prow.astype(jnp.bfloat16)
        qrow = (prow * prow).astype(jnp.bfloat16)
        rate, scale = scale_of(jnp.full((8, 128), width_ref[t, 1], jnp.float32))
        rate = rate[0:1, 0:1]
        near = near_ref[:, :cols]
        pcol = jnp.where(near <= limit, jnp.exp(near * rate) * scale, 0.0)
        pcol_ref[t] = pcol.astype(jnp.bfloat16)
        qcol = (pcol * pcol).astype(jnp.bfloat16)
        denom = jnp.dot(qrow, inv_low, preferred_element_type=jnp.float32).astype(jnp.bfloat16)
        denom = jnp.dot(denom, qcol, preferred_element_type=jnp.float32)
        norm_ref[t] = live_ref[t] / jnp.sqrt(denom)
        for p in range(profiles):
            vec = jnp.zeros((1, wide), jnp.float32)
            for k, term in enumerate(terms):
                if term[3] == p:
                    vec = vec + coeff_ref[t, k] * ring_ref[k : k + 1, :]
            full = jnp.broadcast_to(vec, (wide, wide))
            full = pltpu.roll(full, 0, 1, stride=1, stride_axis=0)
            mats_ref[t, p * wide : (p + 1) * wide, :] = full.astype(jnp.bfloat16)
        return carry

    lax.fori_loop(0, tiles, one, 0)


def convolve_kernel(blocks, slots_ref, part_ref, live_ref, core_ref, *refs):
    own_blocks = refs[:blocks]
    other_blocks = refs[blocks : 2 * blocks]
    (gr_ref, exp_ref, expo_ref, inv_ref, mats_ref) = refs[2 * blocks : 2 * blocks + 5]
    low_ref = refs[2 * blocks + 5]
    out_refs = refs[2 * blocks + 6 : 3 * blocks + 6]
    tile_ref, rows_ref, acc_ref, sem = refs[3 * blocks + 6 :]
    tiles, size, wide = tile_ref.shape
    cols = wide // 2
    owned = own_blocks[0].shape[0]
    profiles = rows_ref.shape[1] // wide
    half = cols // 2

    def copies(t, b):
        slot = slots_ref[t]
        return (
            pltpu.make_async_copy(own_blocks[b].at[slot], tile_ref.at[t, :, pl.ds(0, cols)], sem.at[t, 0]),
            pltpu.make_async_copy(other_blocks[b].at[slot], tile_ref.at[t, :, pl.ds(cols, cols)], sem.at[t, 1]),
        )

    for t in range(tiles):
        for b in range(blocks):
            @pl.when(part_ref[t] == b)
            def _(t=t, b=b):
                for c in copies(t, b):
                    c.start()

    acc_ref[...] = jnp.zeros_like(acc_ref)
    lane = lax.broadcasted_iota(jnp.int32, (size, cols), 1)
    keep = (lane >= half) == (core_ref[0] == 1)

    def one(t, carry):
        for c in copies(t, 0):
            c.wait()
        other = tile_ref[t, :, cols:]
        other = jnp.where(keep, other.astype(jnp.float32), 0.0).astype(jnp.bfloat16)
        tile = jnp.concatenate([tile_ref[t, :, :cols], other], axis=1)
        for p in range(profiles):
            rows_ref[:, p * wide : (p + 1) * wide] = jnp.dot(
                gr_ref[p * size : (p + 1) * size, :], tile, preferred_element_type=jnp.float32
            ).astype(jnp.bfloat16)
        convolved = jnp.dot(rows_ref[...], mats_ref[t], preferred_element_type=jnp.float32)
        own = (exp_ref[t].astype(jnp.float32) - convolved[:, :cols]) * inv_ref[t, :, :cols]
        other = (expo_ref[t].astype(jnp.float32) - convolved[:, cols:]) * inv_ref[t, :, cols:]
        low_ref[t, :, :cols] = own.astype(jnp.bfloat16)
        low_ref[t, :, cols:] = other.astype(jnp.bfloat16)
        where = part_ref[t] * owned + slots_ref[t]
        acc_ref[where] += live_ref[t] * own
        return carry

    lax.fori_loop(0, tiles, one, 0)
    for b in range(blocks):
        out_refs[b][...] = acc_ref[b * owned : (b + 1) * owned].astype(out_refs[b].dtype)


def score_kernel(low_ref, prow_ref, pcol_ref, norm_ref, score_ref):
    tiles = low_ref.shape[0]

    def one(t, carry):
        numer = jnp.dot(prow_ref[t], low_ref[t], preferred_element_type=jnp.float32)
        numer = numer.astype(jnp.bfloat16)
        numer = jnp.dot(numer, pcol_ref[t], preferred_element_type=jnp.float32)
        score_ref[t] = numer * norm_ref[t]
        return carry

    lax.fori_loop(0, tiles, one, 0)


def shape(dims, dtype):
    return jax.ShapeDtypeStruct(dims, dtype)


def vmem(count):
    return [pl.BlockSpec(memory_space=VMEM)] * count


def smem(count):
    return [pl.BlockSpec(memory_space=SMEM)] * count


def anywhere(count):
    return [pl.BlockSpec(memory_space=pl.ANY)] * count


def on_device(templates, exposures, variance, coefficients, psf_width, patch_ids, live_count):
    size = templates.shape[2]
    cols = templates.shape[3]
    owned = templates.shape[1]
    slots = patch_ids.shape[2]
    wide = 2 * cols
    across = lax.axis_size("patch")
    patches_row = owned * across
    blocks = 3 * across
    me = lax.axis_index("patch")
    core = lax.axis_index("band").astype(jnp.int32).reshape(1)
    low = jnp.bfloat16

    own = templates.reshape(owned, size, cols)
    exp_flat = exposures.reshape(-1, size, cols)
    var_flat = variance.reshape(-1, size, cols)
    tiles = exp_flat.shape[0]
    swap = functools.partial(sent, axis="band", distance=1)

    below = shifted(own, "exp", 1)
    above = shifted(own, "exp", -1)
    row = [own] + [fetched(own, "patch", d) for d in range(1, across)]
    rows_below = [below] + [shifted(row[d], "exp", 1) for d in range(1, across)]
    rows_above = [above] + [shifted(row[d], "exp", -1) for d in range(1, across)]
    window = rows_below + row + rows_above
    window_other = [swap(b) for b in window]
    var_other = swap(var_flat)
    exp_other = swap(exp_flat)

    ids = patch_ids.reshape(-1)
    column = ids % patches_row
    shift = (column // owned - me + across) % across
    part = (ids // patches_row) * across + shift
    slot = column % owned
    live = (
        (jnp.arange(slots, dtype=jnp.int32)[None, None, :] < live_count[:, :, None])
        .astype(jnp.float32)
        .reshape(-1)
    )
    coeff = coefficients.reshape(tiles, -1)
    width = psf_width.reshape(tiles, 2)
    gr = jnp.asarray(row_tables(size, HW), dtype=low)
    profiles = gr.shape[0]
    gr = gr.reshape(-1, size)
    ring = jnp.asarray(ring_profiles(wide, HW))

    norm, inv, prow, pcol, mats = pl.pallas_call(
        prepare_kernel,
        name="prepare",
        out_shape=(
            shape((tiles, size, cols), jnp.float32),
            shape((tiles, size, wide), jnp.float32),
            shape((tiles, size, size), low),
            shape((tiles, wide, cols), low),
            shape((tiles, profiles * wide, wide), low),
        ),
        in_specs=smem(4) + vmem(3),
        out_specs=tuple(vmem(5)),
        scratch_shapes=[VMEM((size, size), jnp.float32), VMEM((wide, wide), jnp.float32)],
    )(width, live, core, coeff, ring, var_flat, var_other)

    outs = pl.pallas_call(
        functools.partial(convolve_kernel, blocks),
        name="convolve",
        out_shape=tuple(
            [shape((tiles, size, wide), low)]
            + [
                shape((owned, size, cols), jnp.float32 if b == across else low)
                for b in range(blocks)
            ]
        ),
        in_specs=smem(4) + anywhere(2 * blocks) + vmem(5),
        out_specs=tuple(vmem(1 + blocks)),
        scratch_shapes=[
            VMEM((tiles, size, wide), low),
            VMEM((size, profiles * wide), low),
            VMEM((blocks * owned, size, cols), jnp.float32),
            pltpu.SemaphoreType.DMA((tiles, 2)),
        ],
    )(slot, part, live, core, *window, *window_other, gr, exp_flat, exp_other, inv, mats)
    weighted_low = outs[0]
    parts = outs[1:]

    from_below = [shifted(parts[2 * across + d], "exp", 1) for d in range(across)]
    from_above = [shifted(parts[d], "exp", -1) for d in range(across)]
    total = parts[across] + from_below[0].astype(jnp.float32) + from_above[0].astype(jnp.float32)
    for d in range(1, across):
        merged = (
            parts[across + d].astype(jnp.float32)
            + from_below[d].astype(jnp.float32)
            + from_above[d].astype(jnp.float32)
        ).astype(low)
        total = total + sent(merged, "patch", d).astype(jnp.float32)

    score = pl.pallas_call(
        score_kernel,
        name="score",
        out_shape=shape((tiles, size, cols), jnp.float32),
        in_specs=vmem(4),
        out_specs=vmem(1)[0],
    )(weighted_low, prow, pcol, norm)
    return (total.reshape(1, owned, size, cols), score.reshape(exposures.shape))


def solution(mesh):
    assert mesh.shape["band"] == 2
    in_specs = (
        P(("groups", "exp"), "patch", None, "band"),
        P(("groups", "exp"), "patch", None, None, "band"),
        P(("groups", "exp"), "patch", None, None, "band"),
        P(("groups", "exp"), "patch", None, None),
        P(("groups", "exp"), "patch", None, None),
        P(("groups", "exp"), "patch", None),
        P(("groups", "exp"), "patch"),
    )
    out_specs = (
        P(("groups", "exp"), "patch", None, "band"),
        P(("groups", "exp"), "patch", None, None, "band"),
    )
    return jax.shard_map(
        on_device, mesh=mesh, in_specs=in_specs, out_specs=out_specs, check_vma=False
    )
```

```python
import functools

import jax
import jax.numpy as jnp
import numpy as np
from jax import lax
from jax.experimental import pallas as pl
from jax.experimental.pallas import tpu as pltpu
from jax.sharding import PartitionSpec as P

HW = 10
PW = 7

sigmas = (0.75, 1.5, 3.0)
degrees = (4, 2, 2)

VMEM = pltpu.VMEM
SMEM = pltpu.SMEM


def neighbours(groups, rows):
    if groups % 2 or rows < 2:
        line = [(g * rows + i, g * rows + i + 1) for g in range(groups) for i in range(rows - 1)]
        return line, [(j, i) for i, j in line], False
    ring = []
    for g in range(0, groups, 2):
        loop = [g * rows + i for i in range(rows)] + [(g + 1) * rows + i for i in reversed(range(rows))]
        ring += list(zip(loop, loop[1:] + loop[:1]))
    return ring, [(j, i) for i, j in ring], True


def fetched(block, axis, distance):
    devices = lax.axis_size(axis)
    return lax.ppermute(block, axis, [((i + distance) % devices, i) for i in range(devices)])


def sent(block, axis, distance):
    devices = lax.axis_size(axis)
    return lax.ppermute(block, axis, [(i, (i + distance) % devices) for i in range(devices)])


def basis_terms():
    terms = []
    offset = 0
    for group in range(3):
        for first in range(degrees[group] + 1):
            for second in range(degrees[group] + 1 - first):
                terms.append((group, first, second, offset + first))
        offset = offset + degrees[group] + 1
    return terms


def profile(offset, sigma, power, reach):
    grid = np.arange(-reach, reach + 1).astype(np.float32)
    base = np.exp(-grid * grid / np.float32(2.0 * sigma * sigma)) * (grid / reach) ** power
    scale = np.sqrt(np.sum(base * base))
    spot = offset.astype(np.float32)
    value = np.exp(-spot * spot / np.float32(2.0 * sigma * sigma)) * (spot / reach) ** power / scale
    return np.where(np.abs(offset) <= reach, value, 0.0).astype(np.float32)


def ring_profiles(width, reach):
    lane = np.arange(width)
    offset = np.where(lane < width // 2, lane, lane - width)
    return np.stack([profile(offset, sigmas[t[0]], t[2], reach) for t in basis_terms()])


def row_profiles(reach, rows, lanes):
    offset = np.arange(rows) - reach
    tables = []
    for group in range(3):
        for first in range(degrees[group] + 1):
            tables.append(profile(offset, sigmas[group], first, reach))
    table = np.stack(tables).astype(jnp.bfloat16).astype(np.float32)
    return np.broadcast_to(table[:, :, None], table.shape + (lanes,))


def taps_kernel(core_ref, coeff_ref, ring_ref, spread_ref, band_ref, taps_ref, edge_ref):
    tiles = coeff_ref.shape[0]
    cols = ring_ref.shape[1]
    group = cols // tiles
    reach = HW
    terms = basis_terms()
    profiles = spread_ref.shape[0]
    across = lax.broadcasted_iota(jnp.int32, (cols, cols), 1)
    down = lax.broadcasted_iota(jnp.int32, (cols, cols), 0)
    near = jnp.abs(across - down) <= reach
    same = (across // group) == (down // group)
    count = 2 * reach + 1
    turn = jnp.where(core_ref[0] == 0, group, cols - group)

    def one(t, carry):
        taps = jnp.zeros(taps_ref.shape[1:], jnp.float32)
        for p in range(profiles):
            vec = jnp.zeros((1, cols), jnp.float32)
            for k, term in enumerate(terms):
                if term[3] == p:
                    vec = vec + coeff_ref[t, k] * ring_ref[k : k + 1, :]
            vec = vec.astype(jnp.bfloat16).astype(jnp.float32)
            taps = taps + spread_ref[p] * vec
        taps_ref[t] = taps
        edge_ref[t] = pltpu.roll(taps, turn, 1)
        band_ref[t, 0:cols, :] = jnp.zeros((cols, cols), jnp.bfloat16)
        band_ref[t, (count + 1) * cols :, :] = jnp.zeros((cols, cols), jnp.bfloat16)
        for u in range(count):
            full = jnp.broadcast_to(taps_ref[t, u : u + 1, :], (cols, cols))
            full = pltpu.roll(full, 0, 1, stride=1, stride_axis=0)
            full = jnp.where(near, full, 0.0).astype(jnp.bfloat16)
            band_ref[t, (count - u) * cols : (count - u + 1) * cols, :] = full
        return carry

    lax.fori_loop(0, tiles, one, 0)
    band_ref[tiles, 0:cols, :] = jnp.zeros((cols, cols), jnp.bfloat16)
    band_ref[tiles, (count + 1) * cols :, :] = jnp.zeros((cols, cols), jnp.bfloat16)
    for u in range(count):
        full = jnp.concatenate(
            [jnp.broadcast_to(edge_ref[t, u : u + 1, :], (group, cols)) for t in range(tiles)], axis=0
        )
        full = pltpu.roll(full, 0, 1, stride=1, stride_axis=0)
        full = jnp.where(same, full, 0.0).astype(jnp.bfloat16)
        band_ref[tiles, (count - u) * cols : (count - u + 1) * cols, :] = full


def norms_kernel(width_ref, live_ref, core_ref, own_ref, other_ref,
                 norm_ref, inv_ref, prow_ref, pcol_ref, dist_ref, near_ref):
    tiles, size, cols = own_ref.shape
    wide = 2 * cols
    rows = lax.broadcasted_iota(jnp.int32, (size, size), 0)
    across = lax.broadcasted_iota(jnp.int32, (size, size), 1)
    gap = rows - across
    dist_ref[...] = (gap * gap).astype(jnp.float32)
    inner = lax.broadcasted_iota(jnp.int32, (wide, cols), 0)
    outer = lax.broadcasted_iota(jnp.int32, (wide, cols), 1)
    ring = jnp.abs(inner - outer)
    ring = jnp.minimum(ring, wide - ring)
    near_ref[...] = (ring * ring).astype(jnp.float32)
    lane = lax.broadcasted_iota(jnp.int32, (size, cols), 1)
    keep = (lane >= cols // 2) == (core_ref[0] == 1)
    limit = float(PW * PW)
    spot = lax.broadcasted_iota(jnp.int32, (8, 128), 1)
    spot_low = spot.astype(jnp.float32) - PW

    def table(width, square):
        rate = -0.5 / (width * width)
        base = jnp.where(spot <= 2 * PW, jnp.exp(spot_low * spot_low * rate), 0.0)
        scale = 1.0 / jnp.sum(base[0:1], axis=1, keepdims=True)
        return jnp.where(square <= limit, jnp.exp(square * rate[0:1, 0:1]) * scale, 0.0)

    def one(t, carry):
        inv_own = 1.0 / own_ref[t]
        inv_other = jnp.where(keep, 1.0 / other_ref[t], 0.0)
        inv_ref[t] = inv_own
        inv_low = jnp.concatenate([inv_own, inv_other], axis=1).astype(jnp.bfloat16)
        prow = table(jnp.full((8, 128), width_ref[t, 0], jnp.float32), dist_ref[...])
        prow_ref[t] = prow.astype(jnp.bfloat16)
        qrow = (prow * prow).astype(jnp.bfloat16)
        pcol = table(jnp.full((8, 128), width_ref[t, 1], jnp.float32), near_ref[...])
        pcol_ref[t] = pcol.astype(jnp.bfloat16)
        qcol = (pcol * pcol).astype(jnp.bfloat16)
        denom = jnp.dot(qrow, inv_low, preferred_element_type=jnp.float32).astype(jnp.bfloat16)
        denom = jnp.dot(denom, qcol, preferred_element_type=jnp.float32)
        norm_ref[t] = live_ref[t] / jnp.sqrt(denom)
        return carry

    lax.fori_loop(0, tiles, one, 0)


PAD = 16


def convolve_kernel(blocks, slots_ref, part_ref, live_ref, present_ref, core_ref, *refs):
    own_blocks = refs[:blocks]
    other_blocks = refs[blocks : 2 * blocks]
    (band_ref, exp_ref, inv_ref) = refs[2 * blocks : 2 * blocks + 3]
    low_ref = refs[2 * blocks + 3]
    out_refs = refs[2 * blocks + 4 : 3 * blocks + 4]
    tile_ref, padded_ref, lhs_ref, edge_ref, conv_ref, acc_ref, sem = refs[3 * blocks + 4 :]
    _, tiles, size, cols = tile_ref.shape
    owned = own_blocks[0].shape[0]
    group = cols // tiles
    count = 2 * HW + 2
    first = PAD - HW
    pairs = size // 2

    def copies(t, b):
        slot = slots_ref[t]
        return (
            pltpu.make_async_copy(own_blocks[b].at[slot], tile_ref.at[0, t], sem.at[t, 0]),
            pltpu.make_async_copy(other_blocks[b].at[slot], tile_ref.at[1, t], sem.at[t, 1]),
        )

    for t in range(tiles):
        for b in range(blocks):
            @pl.when(part_ref[t] == b)
            def _(t=t, b=b):
                for c in copies(t, b):
                    c.start()

    acc_ref[...] = jnp.zeros_like(acc_ref)
    padded_ref[0:PAD, :] = jnp.zeros((PAD, cols), jnp.float32)
    padded_ref[PAD + size :, :] = jnp.zeros((PAD, cols), jnp.float32)

    def spread(which):
        for r in range(count):
            lhs_ref[:, r * cols : (r + 1) * cols] = padded_ref[
                pl.ds(first + r, pairs, stride=2), :
            ].astype(jnp.bfloat16)
        weights = jnp.concatenate(
            [band_ref[which, cols:, :], band_ref[which, : count * cols, :]], axis=1
        )
        return jnp.dot(lhs_ref[...], weights, preferred_element_type=jnp.float32)

    lane = lax.broadcasted_iota(jnp.int32, (1, cols), 1)
    start = jnp.where(core_ref[0] == 0, 0, cols - group)
    target = cols - group - start
    strip = jnp.zeros((size, cols), jnp.float32)
    for t in range(tiles):
        copies(t, 0)[1].wait()
        moved = pltpu.roll(tile_ref[1, t].astype(jnp.float32), lax.rem(t * group - start + cols, cols), 1)
        strip = jnp.where(lane // group == t, moved, strip)
    padded_ref[PAD : PAD + size, :] = strip
    edge_ref[...] = spread(tiles)

    def one(t, carry):
        copies(t, 0)[0].wait()
        padded_ref[PAD : PAD + size, :] = tile_ref[0, t].astype(jnp.float32)
        both = spread(t)
        turn = lax.rem(target - t * group + cols, cols)
        for s in range(2):
            edge = pltpu.roll(edge_ref[:, s * cols : (s + 1) * cols], turn, 1)
            edge = jnp.where((lane >= target) & (lane < target + group), edge, 0.0)
            conv_ref[pl.ds(s, pairs, stride=2), :] = both[:, s * cols : (s + 1) * cols] + edge
        convolved = conv_ref[...] * present_ref[t]
        own = (exp_ref[t].astype(jnp.float32) - convolved) * inv_ref[t]
        low_ref[t] = own.astype(jnp.bfloat16)
        where = part_ref[t] * owned + slots_ref[t]
        acc_ref[where] += live_ref[t] * own
        return carry

    lax.fori_loop(0, tiles, one, 0)
    for b in range(blocks):
        out_refs[b][...] = acc_ref[b * owned : (b + 1) * owned].astype(out_refs[b].dtype)


def score_kernel(core_ref, low_ref, other_ref, prow_ref, pcol_ref, norm_ref, score_ref):
    tiles, size, cols = low_ref.shape
    lane = lax.broadcasted_iota(jnp.int32, (size, cols), 1)
    keep = (lane >= cols // 2) == (core_ref[0] == 1)

    def one(t, carry):
        other = jnp.where(keep, other_ref[t].astype(jnp.float32), 0.0).astype(jnp.bfloat16)
        full = jnp.concatenate([low_ref[t], other], axis=1)
        numer = jnp.dot(prow_ref[t], full, preferred_element_type=jnp.float32)
        numer = numer.astype(jnp.bfloat16)
        numer = jnp.dot(numer, pcol_ref[t], preferred_element_type=jnp.float32)
        score_ref[t] = numer * norm_ref[t]
        return carry

    lax.fori_loop(0, tiles, one, 0)


def shape(dims, dtype):
    return jax.ShapeDtypeStruct(dims, dtype)


def vmem(count):
    return [pl.BlockSpec(memory_space=VMEM)] * count


def smem(count):
    return [pl.BlockSpec(memory_space=SMEM)] * count


def anywhere(count):
    return [pl.BlockSpec(memory_space=pl.ANY)] * count


def params(mib):
    return pltpu.CompilerParams(vmem_limit_bytes=mib << 20)


def cost(micros):
    return pl.CostEstimate(flops=int(micros * 1e9), bytes_accessed=int(micros * 3e6), transcendentals=0)


def on_device(templates, exposures, variance, coefficients, psf_width, patch_ids, live_count):
    size = templates.shape[2]
    cols = templates.shape[3]
    owned = templates.shape[1]
    slots = patch_ids.shape[2]
    across = lax.axis_size("patch")
    patches_row = owned * across
    blocks = 3 * across
    me = lax.axis_index("patch")
    row_index = lax.axis_index("exp")
    rows = lax.axis_size("exp")
    core = lax.axis_index("band").astype(jnp.int32).reshape(1)
    low = jnp.bfloat16
    f32 = jnp.float32

    own = templates.reshape(owned, size, cols)
    exp_flat = exposures.reshape(-1, size, cols)
    var_flat = variance.reshape(-1, size, cols)
    tiles = exp_flat.shape[0]
    assert cols % tiles == 0 and cols // tiles >= HW and size % 32 == 0
    swap = functools.partial(sent, axis="band", distance=1)

    forth, back, closed = neighbours(lax.axis_size("groups"), rows)
    flip = lax.axis_index("groups") % 2 if closed else 0
    ahead = lambda block: lax.ppermute(block, ("groups", "exp"), forth)
    behind = lambda block: lax.ppermute(block, ("groups", "exp"), back)
    from_first = jnp.where(flip == 0, row_index > 0, row_index < rows - 1)
    from_last = jnp.where(flip == 0, row_index < rows - 1, row_index > 0)

    row = [own] + [fetched(own, "patch", d) for d in range(1, across)]
    firsts = [ahead(b) for b in row]
    lasts = [behind(b) for b in row]
    window = firsts + row + lasts
    window_other = [swap(b) for b in window]
    var_other = swap(var_flat)

    ids = patch_ids.reshape(-1)
    column = ids % patches_row
    shift = (column // owned - me + across) % across
    step = ids // patches_row
    present = ((row_index + step >= 1) & (row_index + step <= rows)).astype(f32)
    step = jnp.where(flip == 0, step, 2 - step)
    part = step * across + shift
    slot = column % owned
    live = (
        (jnp.arange(slots, dtype=jnp.int32)[None, None, :] < live_count[:, :, None])
        .astype(f32)
        .reshape(-1)
    )
    coeff = coefficients.reshape(tiles, -1)
    width = psf_width.reshape(tiles, 2)
    ring = jnp.asarray(ring_profiles(cols, HW))
    count = 2 * HW + 1
    held = -(-count // 8) * 8
    spread = jnp.asarray(row_profiles(HW, held, cols))

    band = pl.pallas_call(
        taps_kernel,
        name="taps",
        out_shape=shape((tiles + 1, (count + 2) * cols, cols), low),
        in_specs=smem(2) + vmem(2),
        out_specs=vmem(1)[0],
        scratch_shapes=[VMEM((tiles, held, cols), f32), VMEM((tiles, held, cols), f32)],
        compiler_params=params(12),
        cost_estimate=cost(3),
    )(core, coeff, ring, spread)

    norm, inv, prow, pcol = pl.pallas_call(
        norms_kernel,
        name="norms",
        out_shape=(
            shape((tiles, size, cols), f32),
            shape((tiles, size, cols), f32),
            shape((tiles, size, size), low),
            shape((tiles, 2 * cols, cols), low),
        ),
        in_specs=smem(3) + vmem(2),
        out_specs=tuple(vmem(4)),
        scratch_shapes=[VMEM((size, size), f32), VMEM((2 * cols, cols), f32)],
        compiler_params=params(12),
        cost_estimate=cost(5),
    )(width, live, core, var_flat, var_other)

    outs = pl.pallas_call(
        functools.partial(convolve_kernel, blocks),
        name="convolve",
        out_shape=tuple(
            [shape((tiles, size, cols), low)]
            + [shape((owned, size, cols), f32 if b == across else low) for b in range(blocks)]
        ),
        in_specs=smem(5) + anywhere(2 * blocks) + vmem(3),
        out_specs=tuple(vmem(1 + blocks)),
        scratch_shapes=[
            VMEM((2, tiles, size, cols), low),
            VMEM((size + 2 * PAD, cols), f32),
            VMEM((size // 2, (count + 1) * cols), low),
            VMEM((size // 2, 2 * cols), f32),
            VMEM((size, cols), f32),
            VMEM((blocks * owned, size, cols), f32),
            pltpu.SemaphoreType.DMA((tiles, 2)),
        ],
        compiler_params=params(24),
        cost_estimate=cost(5),
    )(slot, part, live, present, core, *window, *window_other, band, exp_flat, inv)
    weighted_low = outs[0]
    parts = outs[1:]

    from_ahead = [ahead(parts[2 * across + d]) for d in reversed(range(across))][::-1]
    from_behind = [behind(parts[d]) for d in reversed(range(across))][::-1]
    weighted_other = swap(weighted_low)

    def received(d):
        one = jnp.where(from_first, from_ahead[d].astype(f32), 0.0)
        return one + jnp.where(from_last, from_behind[d].astype(f32), 0.0)

    total = parts[across]
    for d in range(1, across):
        merged = (parts[across + d].astype(f32) + received(d)).astype(low)
        total = total + sent(merged, "patch", d).astype(f32)
    total = total + received(0)

    score = pl.pallas_call(
        score_kernel,
        name="score",
        out_shape=shape((tiles, size, cols), f32),
        in_specs=smem(1) + vmem(5),
        out_specs=vmem(1)[0],
        compiler_params=params(12),
        cost_estimate=cost(5),
    )(core, weighted_low, weighted_other, prow, pcol, norm)
    return (total.reshape(1, owned, size, cols), score.reshape(exposures.shape))


def solution(mesh):
    assert mesh.shape["band"] == 2
    in_specs = (
        P(("groups", "exp"), "patch", None, "band"),
        P(("groups", "exp"), "patch", None, None, "band"),
        P(("groups", "exp"), "patch", None, None, "band"),
        P(("groups", "exp"), "patch", None, None),
        P(("groups", "exp"), "patch", None, None),
        P(("groups", "exp"), "patch", None),
        P(("groups", "exp"), "patch"),
    )
    out_specs = (
        P(("groups", "exp"), "patch", None, "band"),
        P(("groups", "exp"), "patch", None, None, "band"),
    )
    return jax.shard_map(
        on_device, mesh=mesh, in_specs=in_specs, out_specs=out_specs, check_vma=False
    )
```

```python
import functools

import jax
import jax.numpy as jnp
import numpy as np
from jax import lax
from jax.experimental import pallas as pl
from jax.experimental.pallas import tpu as pltpu
from jax.sharding import PartitionSpec as P


HW = 10
PW = 7

sigmas = (0.75, 1.5, 3.0)
degrees = (4, 2, 2)


VMEM = pltpu.VMEM
SMEM = pltpu.SMEM


def neighbours(groups, rows):
    if groups % 2 or rows < 2:
        line = [(g * rows + i, g * rows + i + 1) for g in range(groups) for i in range(rows - 1)]
        return line, [(j, i) for i, j in line], False
    ring = []
    for g in range(0, groups, 2):
        loop = [g * rows + i for i in range(rows)] + [(g + 1) * rows + i for i in reversed(range(rows))]
        ring += list(zip(loop, loop[1:] + loop[:1]))
    return ring, [(j, i) for i, j in ring], True


def fetched(block, axis, distance):
    devices = lax.axis_size(axis)
    return lax.ppermute(block, axis, [((i + distance) % devices, i) for i in range(devices)])


def sent(block, axis, distance):
    devices = lax.axis_size(axis)
    return lax.ppermute(block, axis, [(i, (i + distance) % devices) for i in range(devices)])


def basis_terms():
    terms = []
    offset = 0
    for group in range(3):
        for first in range(degrees[group] + 1):
            for second in range(degrees[group] + 1 - first):
                terms.append((group, first, second, offset + first))
        offset = offset + degrees[group] + 1
    return terms


def norm_of(sigma, power, reach):
    grid = np.arange(-reach, reach + 1).astype(np.float64)
    base = np.exp(-grid * grid / (2.0 * sigma * sigma)) * (grid / reach) ** power
    return float(1.0 / np.sqrt(np.sum(base * base)))


def profiles_of(offset, reach):
    spot = offset.astype(jnp.float32)
    inside = jnp.abs(offset) <= reach
    tables = []
    for group in range(3):
        base = jnp.where(inside, jnp.exp(spot * spot * (-0.5 / sigmas[group] ** 2)), 0.0)
        for power in range(degrees[group] + 1):
            tables.append(base * norm_of(sigmas[group], power, reach))
            base = base * (spot / reach)
    return tables


def taps_kernel(coeff_ref, band_ref, taps_ref, edge_ref):
    tiles, held, cols = taps_ref.shape
    slots = coeff_ref.shape[2]
    group = cols // tiles
    reach = HW
    terms = basis_terms()
    lane = lax.broadcasted_iota(jnp.int32, (1, cols), 1)
    ring = profiles_of(jnp.where(lane < cols // 2, lane, lane - cols), reach)
    spread = profiles_of(lax.broadcasted_iota(jnp.int32, (held, cols), 0) - reach, reach)
    spread = [table.astype(jnp.bfloat16).astype(jnp.float32) for table in spread]
    starts = [0]
    for degree in degrees:
        starts.append(starts[-1] + degree + 1)
    across = lax.broadcasted_iota(jnp.int32, (cols, cols), 1)
    down = lax.broadcasted_iota(jnp.int32, (cols, cols), 0)
    near = jnp.abs(across - down) <= reach
    same = (across // group) == (down // group)
    count = 2 * reach + 1
    turn = jnp.where(lax.axis_index("band") == 0, group, cols - group)

    def one(t, carry):
        taps = jnp.zeros(taps_ref.shape[1:], jnp.float32)
        for p in range(len(spread)):
            vec = jnp.zeros((1, cols), jnp.float32)
            for k, term in enumerate(terms):
                if term[3] == p:
                    vec = vec + coeff_ref[0, t // slots, t % slots, k] * ring[starts[term[0]] + term[2]]
            vec = vec.astype(jnp.bfloat16).astype(jnp.float32)
            taps = taps + spread[p] * vec
        taps_ref[t] = taps
        edge_ref[t] = pltpu.roll(taps, turn, 1)
        band_ref[t, 0:cols, :] = jnp.zeros((cols, cols), jnp.bfloat16)
        band_ref[t, (count + 1) * cols :, :] = jnp.zeros((cols, cols), jnp.bfloat16)
        for u in range(count):
            full = jnp.broadcast_to(taps_ref[t, u : u + 1, :], (cols, cols))
            full = pltpu.roll(full, 0, 1, stride=1, stride_axis=0)
            full = jnp.where(near, full, 0.0).astype(jnp.bfloat16)
            band_ref[t, (count - u) * cols : (count - u + 1) * cols, :] = full
        return carry

    lax.fori_loop(0, tiles, one, 0)
    band_ref[tiles, 0:cols, :] = jnp.zeros((cols, cols), jnp.bfloat16)
    band_ref[tiles, (count + 1) * cols :, :] = jnp.zeros((cols, cols), jnp.bfloat16)
    for u in range(count):
        full = jnp.concatenate(
            [jnp.broadcast_to(edge_ref[t, u : u + 1, :], (group, cols)) for t in range(tiles)], axis=0
        )
        full = pltpu.roll(full, 0, 1, stride=1, stride_axis=0)
        full = jnp.where(same, full, 0.0).astype(jnp.bfloat16)
        band_ref[tiles, (count - u) * cols : (count - u + 1) * cols, :] = full


def alive(live_ref, t, slots):
    return jnp.where(t % slots < live_ref[0, t // slots], 1.0, 0.0)


def norms_kernel(width_ref, live_ref, own_ref, other_ref,
                 norm_ref, inv_ref, prow_ref, pcol_ref, dist_ref, near_ref):
    tiles, size, cols = own_ref.shape
    wide = 2 * cols
    rows = lax.broadcasted_iota(jnp.int32, (size, size), 0)
    across = lax.broadcasted_iota(jnp.int32, (size, size), 1)
    gap = rows - across
    dist_ref[...] = (gap * gap).astype(jnp.float32)
    inner = lax.broadcasted_iota(jnp.int32, (wide, cols), 0)
    outer = lax.broadcasted_iota(jnp.int32, (wide, cols), 1)
    ring = jnp.abs(inner - outer)
    ring = jnp.minimum(ring, wide - ring)
    near_ref[...] = (ring * ring).astype(jnp.float32)
    lane = lax.broadcasted_iota(jnp.int32, (size, cols), 1)
    keep = (lane >= cols // 2) == (lax.axis_index("band") == 1)
    slots = width_ref.shape[3]
    limit = float(PW * PW)
    spot = lax.broadcasted_iota(jnp.int32, (8, 128), 1)
    spot_low = spot.astype(jnp.float32) - PW

    def table(width, square):
        rate = -0.5 / (width * width)
        base = jnp.where(spot <= 2 * PW, jnp.exp(spot_low * spot_low * rate), 0.0)
        scale = 1.0 / jnp.sum(base[0:1], axis=1, keepdims=True)
        return jnp.where(square <= limit, jnp.exp(square * rate[0:1, 0:1]) * scale, 0.0)

    def one(t, carry):
        inv_own = 1.0 / own_ref[t]
        inv_other = jnp.where(keep, 1.0 / other_ref[t], 0.0)
        inv_ref[t] = inv_own
        inv_low = jnp.concatenate([inv_own, inv_other], axis=1).astype(jnp.bfloat16)
        prow = table(jnp.full((8, 128), width_ref[0, t // slots, 0, t % slots], jnp.float32), dist_ref[...])
        prow_ref[t] = prow.astype(jnp.bfloat16)
        qrow = (prow * prow).astype(jnp.bfloat16)
        pcol = table(jnp.full((8, 128), width_ref[0, t // slots, 1, t % slots], jnp.float32), near_ref[...])
        pcol_ref[t] = pcol.astype(jnp.bfloat16)
        qcol = (pcol * pcol).astype(jnp.bfloat16)
        denom = jnp.dot(qrow, inv_low, preferred_element_type=jnp.float32).astype(jnp.bfloat16)
        denom = jnp.dot(denom, qcol, preferred_element_type=jnp.float32)
        norm_ref[t] = alive(live_ref, t, slots) / jnp.sqrt(denom)
        return carry

    lax.fori_loop(0, tiles, one, 0)


PAD = 16


def convolve_kernel(blocks, closed, ids_ref, live_ref, *refs):
    own_blocks = refs[:blocks]
    other_blocks = refs[blocks : 2 * blocks]
    (band_ref, exp_ref, inv_ref) = refs[2 * blocks : 2 * blocks + 3]
    low_ref = refs[2 * blocks + 3]
    out_refs = refs[2 * blocks + 4 : 3 * blocks + 4]
    tile_ref, padded_ref, lhs_ref, edge_ref, conv_ref, acc_ref, sem = refs[3 * blocks + 4 :]
    _, tiles, size, cols = tile_ref.shape
    owned = own_blocks[0].shape[0]
    group = cols // tiles
    count = 2 * HW + 2
    first = PAD - HW
    pairs = size // 2

    slots = ids_ref.shape[2]
    core = lax.axis_index("band")
    row = lax.axis_index("exp")
    rows = lax.axis_size("exp")
    columns = lax.axis_size("patch")
    flip = lax.rem(lax.axis_index("groups"), 2) if closed else 0

    def place(t):
        name = ids_ref[0, t // slots, t % slots]
        step = name // (owned * columns)
        column = name - step * (owned * columns)
        owner = column // owned
        shift = lax.rem(owner - lax.axis_index("patch") + columns, columns)
        inside = (row + step >= 1) & (row + step <= rows)
        step = jnp.where(flip == 0, step, 2 - step)
        return step * columns + shift, column - owner * owned, jnp.where(inside, 1.0, 0.0)

    def copies(t, b, slot=0):
        return (
            pltpu.make_async_copy(own_blocks[b].at[slot], tile_ref.at[0, t], sem.at[t, 0]),
            pltpu.make_async_copy(other_blocks[b].at[slot], tile_ref.at[1, t], sem.at[t, 1]),
        )

    for t in range(tiles):
        part, slot, _ = place(t)
        for b in range(blocks):
            @pl.when(part == b)
            def _(t=t, b=b, slot=slot):
                for c in copies(t, b, slot):
                    c.start()

    acc_ref[...] = jnp.zeros_like(acc_ref)
    padded_ref[0:PAD, :] = jnp.zeros((PAD, cols), jnp.float32)
    padded_ref[PAD + size :, :] = jnp.zeros((PAD, cols), jnp.float32)

    def spread(which):
        for r in range(count):
            lhs_ref[:, r * cols : (r + 1) * cols] = padded_ref[
                pl.ds(first + r, pairs, stride=2), :
            ].astype(jnp.bfloat16)
        weights = jnp.concatenate(
            [band_ref[which, cols:, :], band_ref[which, : count * cols, :]], axis=1
        )
        return jnp.dot(lhs_ref[...], weights, preferred_element_type=jnp.float32)

    lane = lax.broadcasted_iota(jnp.int32, (1, cols), 1)
    start = jnp.where(core == 0, 0, cols - group)
    target = cols - group - start
    strip = jnp.zeros((size, cols), jnp.float32)
    for t in range(tiles):
        copies(t, 0)[1].wait()
        moved = pltpu.roll(tile_ref[1, t].astype(jnp.float32), lax.rem(t * group - start + cols, cols), 1)
        strip = jnp.where(lane // group == t, moved, strip)
    padded_ref[PAD : PAD + size, :] = strip
    edge_ref[...] = spread(tiles)

    def one(t, carry):
        copies(t, 0)[0].wait()
        padded_ref[PAD : PAD + size, :] = tile_ref[0, t].astype(jnp.float32)
        both = spread(t)
        turn = lax.rem(target - t * group + cols, cols)
        for s in range(2):
            edge = pltpu.roll(edge_ref[:, s * cols : (s + 1) * cols], turn, 1)
            edge = jnp.where((lane >= target) & (lane < target + group), edge, 0.0)
            conv_ref[pl.ds(s, pairs, stride=2), :] = both[:, s * cols : (s + 1) * cols] + edge
        part, slot, present = place(t)
        convolved = conv_ref[...] * present
        own = (exp_ref[t].astype(jnp.float32) - convolved) * inv_ref[t]
        low_ref[t] = own.astype(jnp.bfloat16)
        acc_ref[part * owned + slot] += alive(live_ref, t, slots) * own
        return carry

    lax.fori_loop(0, tiles, one, 0)
    for b in range(blocks):
        out_refs[b][...] = acc_ref[b * owned : (b + 1) * owned].astype(out_refs[b].dtype)


def score_kernel(low_ref, other_ref, prow_ref, pcol_ref, norm_ref, score_ref):
    tiles, size, cols = low_ref.shape
    lane = lax.broadcasted_iota(jnp.int32, (size, cols), 1)
    keep = (lane >= cols // 2) == (lax.axis_index("band") == 1)

    def one(t, carry):
        other = jnp.where(keep, other_ref[t].astype(jnp.float32), 0.0).astype(jnp.bfloat16)
        full = jnp.concatenate([low_ref[t], other], axis=1)
        numer = jnp.dot(prow_ref[t], full, preferred_element_type=jnp.float32)
        numer = numer.astype(jnp.bfloat16)
        numer = jnp.dot(numer, pcol_ref[t], preferred_element_type=jnp.float32)
        score_ref[t] = numer * norm_ref[t]
        return carry

    lax.fori_loop(0, tiles, one, 0)


def merge_kernel(closed, here_ref, first_ref, last_ref, *refs):
    row = lax.axis_index("exp")
    rows = lax.axis_size("exp")
    flip = lax.rem(lax.axis_index("groups"), 2) if closed else 0
    has_first = jnp.where(flip == 0, row > 0, row < rows - 1)
    has_last = jnp.where(flip == 0, row < rows - 1, row > 0)
    out_ref = refs[-1]
    owned, size, _ = out_ref.shape
    chunk = size // 4

    def one(i, carry):
        at = (i // 4, pl.ds(pl.multiple_of(i % 4 * chunk, chunk), chunk))
        total = here_ref[at].astype(jnp.float32)
        total = total + jnp.where(has_first, first_ref[at].astype(jnp.float32), 0.0)
        total = total + jnp.where(has_last, last_ref[at].astype(jnp.float32), 0.0)
        for ref in refs[:-1]:
            total = total + ref[at].astype(jnp.float32)
        out_ref[at] = total.astype(out_ref.dtype)
        return carry

    lax.fori_loop(0, owned * 4, one, 0)


def shape(dims, dtype):
    return jax.ShapeDtypeStruct(dims, dtype)


def vmem(count):
    return [pl.BlockSpec(memory_space=VMEM)] * count


def smem(count):
    return [pl.BlockSpec(memory_space=SMEM)] * count


def anywhere(count):
    return [pl.BlockSpec(memory_space=pl.ANY)] * count


def params(mib):
    return pltpu.CompilerParams(vmem_limit_bytes=mib << 20)


def cost(micros):
    return pl.CostEstimate(flops=int(micros * 1e9), bytes_accessed=int(micros * 3e6), transcendentals=0)


def on_device(templates, exposures, variance, coefficients, psf_width, patch_ids, live_count):
    size = templates.shape[2]
    cols = templates.shape[3]
    owned = templates.shape[1]
    across = lax.axis_size("patch")
    blocks = 3 * across
    low = jnp.bfloat16
    f32 = jnp.float32

    own = templates.reshape(owned, size, cols)
    exp_flat = exposures.reshape(-1, size, cols)
    var_flat = variance.reshape(-1, size, cols)
    tiles = exp_flat.shape[0]
    assert cols % tiles == 0 and cols // tiles >= HW and size % 32 == 0
    swap = functools.partial(sent, axis="band", distance=1)

    forth, back, closed = neighbours(lax.axis_size("groups"), lax.axis_size("exp"))
    ahead = lambda block: lax.ppermute(block, ("groups", "exp"), forth)
    behind = lambda block: lax.ppermute(block, ("groups", "exp"), back)
    row = [own] + [fetched(own, "patch", d) for d in range(1, across)]
    firsts = [ahead(own)]
    lasts = [behind(own)]
    var_other = swap(var_flat)

    count = 2 * HW + 1
    held = -(-count // 8) * 8
    band = pl.pallas_call(
        taps_kernel,
        name="taps",
        out_shape=shape((tiles + 1, (count + 2) * cols, cols), low),
        in_specs=smem(1),
        out_specs=vmem(1)[0],
        scratch_shapes=[VMEM((tiles, held, cols), f32), VMEM((tiles, held, cols), f32)],
        compiler_params=params(4),
        cost_estimate=cost(3),
    )(coefficients)
    band, row = lax.optimization_barrier((band, row))
    firsts += [ahead(row[d]) for d in range(1, across)]
    lasts += [behind(row[d]) for d in range(1, across)]

    norm, inv, prow, pcol = pl.pallas_call(
        norms_kernel,
        name="norms",
        out_shape=(
            shape((tiles, size, cols), f32),
            shape((tiles, size, cols), f32),
            shape((tiles, size, size), low),
            shape((tiles, 2 * cols, cols), low),
        ),
        in_specs=smem(2) + vmem(2),
        out_specs=tuple(vmem(4)),
        scratch_shapes=[VMEM((size, size), f32), VMEM((2 * cols, cols), f32)],
        compiler_params=params(6),
        cost_estimate=cost(5),
    )(jnp.swapaxes(psf_width, 2, 3), live_count, var_flat, var_other)
    early = [swap(b) for b in [firsts[0]] + row + [lasts[0]]]
    inv, firsts[1:], lasts[1:] = lax.optimization_barrier((inv, firsts[1:], lasts[1:]))
    window = firsts + row + lasts
    window_other = early[:1] + [swap(b) for b in firsts[1:]] + early[1:-1]
    window_other = window_other + early[-1:] + [swap(b) for b in lasts[1:]]

    outs = pl.pallas_call(
        functools.partial(convolve_kernel, blocks, closed),
        name="convolve",
        out_shape=tuple(
            [shape((tiles, size, cols), low)]
            + [shape((owned, size, cols), f32 if b == across else low) for b in range(blocks)]
        ),
        in_specs=smem(2) + anywhere(2 * blocks) + vmem(3),
        out_specs=tuple(vmem(1 + blocks)),
        scratch_shapes=[
            VMEM((2, tiles, size, cols), low),
            VMEM((size + 2 * PAD, cols), f32),
            VMEM((size // 2, (count + 1) * cols), low),
            VMEM((size // 2, 2 * cols), f32),
            VMEM((size, cols), f32),
            VMEM((blocks * owned, size, cols), f32),
            pltpu.SemaphoreType.DMA((tiles, 2)),
        ],
        compiler_params=params(12),
        cost_estimate=cost(5),
    )(patch_ids, live_count, *window, *window_other, band, exp_flat, inv)
    weighted_low = outs[0]
    parts = outs[1:]

    weighted_other = swap(weighted_low)
    from_ahead = [ahead(parts[2 * across + d]) for d in range(across)]
    from_behind = [behind(parts[d]) for d in range(across)]
    score = pl.pallas_call(
        score_kernel,
        name="score",
        out_shape=shape((tiles, size, cols), f32),
        in_specs=vmem(5),
        out_specs=vmem(1)[0],
        compiler_params=params(4),
        cost_estimate=cost(5),
    )(weighted_low, weighted_other, prow, pcol, norm)
    score, from_ahead[1:], from_behind[1:] = lax.optimization_barrier(
        (score, from_ahead[1:], from_behind[1:])
    )

    def merge(dtype, *arrays):
        return pl.pallas_call(
            functools.partial(merge_kernel, closed),
            name="merge",
            out_shape=shape((owned, size, cols), dtype),
            in_specs=vmem(len(arrays)),
            out_specs=vmem(1)[0],
            compiler_params=params(2),
            cost_estimate=cost(0.5),
        )(*arrays)

    come = []
    for d in range(1, across):
        merged = merge(low, parts[across + d], from_ahead[d], from_behind[d])
        come.append(sent(merged, "patch", d))
    total = merge(f32, parts[across], from_ahead[0], from_behind[0], *come)
    return (total.reshape(1, owned, size, cols), score.reshape(exposures.shape))


def solution(mesh):
    assert mesh.shape["band"] == 2
    in_specs = (
        P(("groups", "exp"), "patch", None, "band"),
        P(("groups", "exp"), "patch", None, None, "band"),
        P(("groups", "exp"), "patch", None, None, "band"),
        P(("groups", "exp"), "patch", None, None),
        P(("groups", "exp"), "patch", None, None),
        P(("groups", "exp"), "patch", None),
        P(("groups", "exp"), "patch"),
    )
    out_specs = (
        P(("groups", "exp"), "patch", None, "band"),
        P(("groups", "exp"), "patch", None, None, "band"),
    )

    def step(*args):
        return on_device(*args)

    step = jax.shard_map(step, mesh=mesh, in_specs=in_specs, out_specs=out_specs, check_vma=False)
    return step
```

```python
import functools

import jax
import jax.numpy as jnp
import numpy as np
from jax import lax
from jax.experimental import pallas as pl
from jax.experimental.pallas import tpu as pltpu
from jax.sharding import PartitionSpec as P


HW = 10
PW = 7

sigmas = (0.75, 1.5, 3.0)
degrees = (4, 2, 2)


VMEM = pltpu.VMEM
SMEM = pltpu.SMEM


def neighbours(groups, rows):
    if groups % 2 or rows < 2:
        line = [(g * rows + i, g * rows + i + 1) for g in range(groups) for i in range(rows - 1)]
        return line, [(j, i) for i, j in line], False
    ring = []
    for g in range(0, groups, 2):
        loop = [g * rows + i for i in range(rows)] + [(g + 1) * rows + i for i in reversed(range(rows))]
        ring += list(zip(loop, loop[1:] + loop[:1]))
    return ring, [(j, i) for i, j in ring], True


def fetched(block, axis, distance):
    devices = lax.axis_size(axis)
    return lax.ppermute(block, axis, [((i + distance) % devices, i) for i in range(devices)])


def sent(block, axis, distance):
    devices = lax.axis_size(axis)
    return lax.ppermute(block, axis, [(i, (i + distance) % devices) for i in range(devices)])


def basis_terms():
    terms = []
    offset = 0
    for group in range(3):
        for first in range(degrees[group] + 1):
            for second in range(degrees[group] + 1 - first):
                terms.append((group, first, second, offset + first))
        offset = offset + degrees[group] + 1
    return terms


def norm_of(sigma, power, reach):
    grid = np.arange(-reach, reach + 1).astype(np.float64)
    base = np.exp(-grid * grid / (2.0 * sigma * sigma)) * (grid / reach) ** power
    return float(1.0 / np.sqrt(np.sum(base * base)))


def profiles_of(offset, reach):
    spot = offset.astype(jnp.float32)
    inside = jnp.abs(offset) <= reach
    tables = []
    for group in range(3):
        base = jnp.where(inside, jnp.exp(spot * spot * (-0.5 / sigmas[group] ** 2)), 0.0)
        for power in range(degrees[group] + 1):
            tables.append(base * norm_of(sigmas[group], power, reach))
            base = base * (spot / reach)
    return tables


def taps_kernel(coeff_ref, band_ref, taps_ref, edge_ref):
    tiles, held, cols = taps_ref.shape
    slots = coeff_ref.shape[2]
    group = cols // tiles
    reach = HW
    terms = basis_terms()
    lane = lax.broadcasted_iota(jnp.int32, (1, cols), 1)
    ring = profiles_of(jnp.where(lane < cols // 2, lane, lane - cols), reach)
    spread = profiles_of(lax.broadcasted_iota(jnp.int32, (held, cols), 0) - reach, reach)
    spread = [table.astype(jnp.bfloat16).astype(jnp.float32) for table in spread]
    starts = [0]
    for degree in degrees:
        starts.append(starts[-1] + degree + 1)
    across = lax.broadcasted_iota(jnp.int32, (cols, cols), 1)
    down = lax.broadcasted_iota(jnp.int32, (cols, cols), 0)
    near = jnp.abs(across - down) <= reach
    same = (across // group) == (down // group)
    count = 2 * reach + 1
    turn = jnp.where(lax.axis_index("band") == 0, group, cols - group)

    def one(t, carry):
        taps = jnp.zeros(taps_ref.shape[1:], jnp.float32)
        for p in range(len(spread)):
            vec = jnp.zeros((1, cols), jnp.float32)
            for k, term in enumerate(terms):
                if term[3] == p:
                    vec = vec + coeff_ref[0, t // slots, t % slots, k] * ring[starts[term[0]] + term[2]]
            vec = vec.astype(jnp.bfloat16).astype(jnp.float32)
            taps = taps + spread[p] * vec
        taps_ref[t] = taps
        edge_ref[t] = pltpu.roll(taps, turn, 1)
        band_ref[t, 0:cols, :] = jnp.zeros((cols, cols), jnp.bfloat16)
        band_ref[t, (count + 1) * cols :, :] = jnp.zeros((cols, cols), jnp.bfloat16)
        for u in range(count):
            full = jnp.broadcast_to(taps_ref[t, u : u + 1, :], (cols, cols))
            full = pltpu.roll(full, 0, 1, stride=1, stride_axis=0)
            full = jnp.where(near, full, 0.0).astype(jnp.bfloat16)
            band_ref[t, (count - u) * cols : (count - u + 1) * cols, :] = full
        return carry

    lax.fori_loop(0, tiles, one, 0, unroll=tiles)
    band_ref[tiles, 0:cols, :] = jnp.zeros((cols, cols), jnp.bfloat16)
    band_ref[tiles, (count + 1) * cols :, :] = jnp.zeros((cols, cols), jnp.bfloat16)
    for u in range(count):
        full = jnp.concatenate(
            [jnp.broadcast_to(edge_ref[t, u : u + 1, :], (group, cols)) for t in range(tiles)], axis=0
        )
        full = pltpu.roll(full, 0, 1, stride=1, stride_axis=0)
        full = jnp.where(same, full, 0.0).astype(jnp.bfloat16)
        band_ref[tiles, (count - u) * cols : (count - u + 1) * cols, :] = full


def alive(live_ref, t, slots):
    return jnp.where(t % slots < live_ref[0, t // slots], 1.0, 0.0)


def norms_kernel(width_ref, live_ref, own_ref, other_ref,
                 norm_ref, prow_ref, pcol_ref, dist_ref, near_ref):
    tiles, size, cols = own_ref.shape
    wide = 2 * cols
    rows = lax.broadcasted_iota(jnp.int32, (size, size), 0)
    across = lax.broadcasted_iota(jnp.int32, (size, size), 1)
    gap = rows - across
    dist_ref[...] = (gap * gap).astype(jnp.float32)
    inner = lax.broadcasted_iota(jnp.int32, (wide, cols), 0)
    outer = lax.broadcasted_iota(jnp.int32, (wide, cols), 1)
    ring = jnp.abs(inner - outer)
    ring = jnp.minimum(ring, wide - ring)
    near_ref[...] = (ring * ring).astype(jnp.float32)
    lane = lax.broadcasted_iota(jnp.int32, (size, cols), 1)
    keep = (lane >= cols // 2) == (lax.axis_index("band") == 1)
    slots = width_ref.shape[3]
    limit = float(PW * PW)
    spot = lax.broadcasted_iota(jnp.int32, (8, 128), 1)
    spot_low = spot.astype(jnp.float32) - PW

    def table(width, square):
        rate = -0.5 / (width * width)
        base = jnp.where(spot <= 2 * PW, jnp.exp(spot_low * spot_low * rate), 0.0)
        scale = 1.0 / jnp.sum(base[0:1], axis=1, keepdims=True)
        return jnp.where(square <= limit, jnp.exp(square * rate[0:1, 0:1]) * scale, 0.0)

    def one(t, carry):
        inv_own = 1.0 / own_ref[t]
        inv_other = jnp.where(keep, 1.0 / other_ref[t], 0.0)
        inv_low = jnp.concatenate([inv_own, inv_other], axis=1).astype(jnp.bfloat16)
        prow = table(jnp.full((8, 128), width_ref[0, t // slots, 0, t % slots], jnp.float32), dist_ref[...])
        prow_ref[t] = prow.astype(jnp.bfloat16)
        qrow = (prow * prow).astype(jnp.bfloat16)
        pcol = table(jnp.full((8, 128), width_ref[0, t // slots, 1, t % slots], jnp.float32), near_ref[...])
        pcol_ref[t] = pcol.astype(jnp.bfloat16)
        qcol = (pcol * pcol).astype(jnp.bfloat16)
        denom = jnp.dot(qrow, inv_low, preferred_element_type=jnp.float32).astype(jnp.bfloat16)
        denom = jnp.dot(denom, qcol, preferred_element_type=jnp.float32)
        norm_ref[t] = alive(live_ref, t, slots) / jnp.sqrt(denom)
        return carry

    lax.fori_loop(0, tiles, one, 0, unroll=tiles)


PAD = 16


def convolve_kernel(blocks, closed, pieces, ids_ref, live_ref, *refs):
    own_blocks = refs[:blocks]
    other_blocks = refs[blocks : 2 * blocks]
    (band_ref, exp_ref, var_ref) = refs[2 * blocks : 2 * blocks + 3]
    low_ref = refs[2 * blocks + 3]
    out_refs = refs[2 * blocks + 4 : 2 * blocks + 4 + len(pieces)]
    tile_ref, padded_ref, lhs_ref, edge_ref, conv_ref, acc_ref = refs[2 * blocks + 4 + len(pieces) :]
    _, tiles, size, cols = tile_ref.shape
    owned = own_blocks[0].shape[0]
    group = cols // tiles
    count = 2 * HW + 2
    first = PAD - HW
    pairs = size // 2
    side = padded_ref.shape[0]

    slots = ids_ref.shape[2]
    core = lax.axis_index("band")
    row = lax.axis_index("exp")
    rows = lax.axis_size("exp")
    columns = lax.axis_size("patch")
    flip = lax.rem(lax.axis_index("groups"), 2) if closed else 0

    def place(t):
        name = ids_ref[0, t // slots, t % slots]
        step = name // (owned * columns)
        column = name - step * (owned * columns)
        owner = column // owned
        shift = lax.rem(owner - lax.axis_index("patch") + columns, columns)
        inside = (row + step >= 1) & (row + step <= rows)
        step = jnp.where(flip == 0, step, 2 - step)
        return step * columns + shift, column - owner * owned, jnp.where(inside, 1.0, 0.0)

    for t in range(tiles):
        part, slot, _ = place(t)
        for b in range(blocks):
            @pl.when(part == b)
            def _(t=t, b=b, slot=slot):
                tile_ref[0, t] = own_blocks[b][slot]
                tile_ref[1, t] = other_blocks[b][slot]

    acc_ref[...] = jnp.zeros_like(acc_ref)
    for n in range(side):
        padded_ref[n, 0:PAD, :] = jnp.zeros((PAD, cols), jnp.float32)
        padded_ref[n, PAD + size :, :] = jnp.zeros((PAD, cols), jnp.float32)

    def build(n):
        for r in range(count):
            lhs_ref[n, :, r * cols : (r + 1) * cols] = padded_ref[
                n, pl.ds(first + r, pairs, stride=2), :
            ].astype(jnp.bfloat16)

    def spread(n, which):
        weights = jnp.concatenate(
            [band_ref[which, cols:, :], band_ref[which, : count * cols, :]], axis=1
        )
        return jnp.dot(lhs_ref[n], weights, preferred_element_type=jnp.float32)

    lane = lax.broadcasted_iota(jnp.int32, (1, cols), 1)
    start = jnp.where(core == 0, 0, cols - group)
    target = cols - group - start
    strip = jnp.zeros((size, cols), jnp.float32)
    for t in range(tiles):
        moved = pltpu.roll(tile_ref[1, t].astype(jnp.float32), lax.rem(t * group - start + cols, cols), 1)
        strip = jnp.where(lane // group == t, moved, strip)
    padded_ref[0, PAD : PAD + size, :] = strip
    build(0)
    edge_ref[...] = spread(0, tiles)

    def some(i, carry):
        for n in range(side):
            padded_ref[n, PAD : PAD + size, :] = tile_ref[0, i * side + n].astype(jnp.float32)
            build(n)
        both = [spread(n, i * side + n) for n in range(side)]
        for n in range(side):
            t = i * side + n
            turn = lax.rem(target - t * group + cols, cols)
            for s in range(2):
                edge = pltpu.roll(edge_ref[:, s * cols : (s + 1) * cols], turn, 1)
                edge = jnp.where((lane >= target) & (lane < target + group), edge, 0.0)
                conv_ref[n, pl.ds(s, pairs, stride=2), :] = both[n][:, s * cols : (s + 1) * cols] + edge
            part, slot, present = place(t)
            convolved = conv_ref[n] * present
            own = (exp_ref[t].astype(jnp.float32) - convolved) * (1.0 / var_ref[t])
            low_ref[t] = own.astype(jnp.bfloat16)
            acc_ref[part * owned + slot] += alive(live_ref, t, slots) * own
        return carry

    lax.fori_loop(0, tiles // side, some, 0)
    for ref, (b, begin, end) in zip(out_refs, pieces):
        ref[...] = acc_ref[b * owned + begin : b * owned + end].astype(ref.dtype)


def score_kernel(low_ref, other_ref, prow_ref, pcol_ref, norm_ref, score_ref):
    tiles, size, cols = low_ref.shape
    lane = lax.broadcasted_iota(jnp.int32, (size, cols), 1)
    keep = (lane >= cols // 2) == (lax.axis_index("band") == 1)

    def one(t, carry):
        other = jnp.where(keep, other_ref[t].astype(jnp.float32), 0.0).astype(jnp.bfloat16)
        full = jnp.concatenate([low_ref[t], other], axis=1)
        numer = jnp.dot(prow_ref[t], full, preferred_element_type=jnp.float32)
        numer = numer.astype(jnp.bfloat16)
        numer = jnp.dot(numer, pcol_ref[t], preferred_element_type=jnp.float32)
        score_ref[t] = numer * norm_ref[t]
        return carry

    lax.fori_loop(0, tiles, one, 0, unroll=tiles)


def merge_kernel(closed, here_ref, first_ref, last_ref, *refs):
    row = lax.axis_index("exp")
    rows = lax.axis_size("exp")
    flip = lax.rem(lax.axis_index("groups"), 2) if closed else 0
    has_first = jnp.where(flip == 0, row > 0, row < rows - 1)
    has_last = jnp.where(flip == 0, row < rows - 1, row > 0)
    out_ref, made_ref, sem = refs[-3:]
    come = refs[:-3]
    owned = here_ref.shape[0]
    cuts = halves(owned)
    moves = []
    for patch in range(owned):
        total = here_ref[patch].astype(jnp.float32)
        total = total + jnp.where(has_first, first_ref[patch].astype(jnp.float32), 0.0)
        total = total + jnp.where(has_last, last_ref[patch].astype(jnp.float32), 0.0)
        for n, ref in enumerate(come):
            begin, end = cuts[n % len(cuts)]
            if begin <= patch < end:
                total = total + ref[patch - begin].astype(jnp.float32)
        if not come:
            out_ref[patch] = total.astype(out_ref.dtype)
        else:
            made_ref[patch] = total
            moves.append(pltpu.make_async_copy(made_ref.at[patch], out_ref.at[patch], sem.at[patch]))
            moves[-1].start()
    for move in moves:
        move.wait()


def halves(count):
    return [(0, count // 2), (count // 2, count)] if count % 2 == 0 else [(0, count)]


def shape(dims, dtype):
    return jax.ShapeDtypeStruct(dims, dtype)


def vmem(count):
    return [pl.BlockSpec(memory_space=VMEM)] * count


def smem(count):
    return [pl.BlockSpec(memory_space=SMEM)] * count


def params(mib):
    return pltpu.CompilerParams(vmem_limit_bytes=mib << 20)


def cost(micros):
    return pl.CostEstimate(flops=int(micros * 1e9), bytes_accessed=int(micros * 3e6), transcendentals=0)


def on_device(templates, exposures, variance, coefficients, psf_width, patch_ids, live_count):
    size = templates.shape[2]
    cols = templates.shape[3]
    owned = templates.shape[1]
    across = lax.axis_size("patch")
    blocks = 3 * across
    low = jnp.bfloat16
    f32 = jnp.float32

    own = templates.reshape(owned, size, cols)
    exp_flat = exposures.reshape(-1, size, cols)
    var_flat = variance.reshape(-1, size, cols)
    tiles = exp_flat.shape[0]
    assert cols % tiles == 0 and cols // tiles >= HW and size % 32 == 0
    swap = functools.partial(sent, axis="band", distance=1)

    forth, back, closed = neighbours(lax.axis_size("groups"), lax.axis_size("exp"))
    ahead = lambda block: lax.ppermute(block, ("groups", "exp"), forth)
    behind = lambda block: lax.ppermute(block, ("groups", "exp"), back)
    row = [own] + [fetched(own, "patch", d) for d in range(1, across)]
    firsts = [ahead(own)]
    lasts = [behind(own)]
    var_other = swap(var_flat)

    count = 2 * HW + 1
    held = -(-count // 8) * 8
    band = pl.pallas_call(
        taps_kernel,
        name="taps",
        out_shape=shape((tiles + 1, (count + 2) * cols, cols), low),
        in_specs=smem(1),
        out_specs=vmem(1)[0],
        scratch_shapes=[VMEM((tiles, held, cols), f32), VMEM((tiles, held, cols), f32)],
        compiler_params=params(4),
        cost_estimate=cost(3),
    )(coefficients)
    band, row = lax.optimization_barrier((band, row))
    firsts += [ahead(row[d]) for d in range(1, across)]
    lasts += [behind(row[d]) for d in range(1, across)]

    norm, prow, pcol = pl.pallas_call(
        norms_kernel,
        name="norms",
        out_shape=(
            shape((tiles, size, cols), f32),
            shape((tiles, size, size), low),
            shape((tiles, 2 * cols, cols), low),
        ),
        in_specs=smem(2) + vmem(2),
        out_specs=tuple(vmem(3)),
        scratch_shapes=[VMEM((size, size), f32), VMEM((2 * cols, cols), f32)],
        compiler_params=params(6),
        cost_estimate=cost(5),
    )(jnp.swapaxes(psf_width, 2, 3), live_count, var_flat, var_other)
    norm, firsts[1:], lasts[1:] = lax.optimization_barrier((norm, firsts[1:], lasts[1:]))
    early = [swap(b) for b in [firsts[0]] + row + [lasts[0]]]
    window = firsts + row + lasts
    window_other = early[:1] + [swap(b) for b in firsts[1:]] + early[1:-1]
    window_other = window_other + early[-1:] + [swap(b) for b in lasts[1:]]

    side = 2 if tiles % 2 == 0 else 1
    cuts = halves(owned)
    pieces = [(b, 0, owned) for b in (0, across, 2 * across)]
    pieces += [(n * across + d, *cut) for d in range(1, across) for cut in cuts for n in range(3)]
    outs = pl.pallas_call(
        functools.partial(convolve_kernel, blocks, closed, pieces),
        name="convolve",
        out_shape=tuple(
            [shape((tiles, size, cols), low)]
            + [shape((e - a, size, cols), f32 if b == across else low) for b, a, e in pieces]
        ),
        in_specs=smem(2) + vmem(2 * blocks + 3),
        out_specs=tuple(vmem(1 + len(pieces))),
        scratch_shapes=[
            VMEM((2, tiles, size, cols), low),
            VMEM((side, size + 2 * PAD, cols), f32),
            VMEM((side, size // 2, (count + 1) * cols), low),
            VMEM((size // 2, 2 * cols), f32),
            VMEM((side, size, cols), f32),
            VMEM((blocks * owned, size, cols), f32),
        ],
        compiler_params=params(12),
        cost_estimate=cost(5),
    )(patch_ids, live_count, *window, *window_other, band, exp_flat, var_flat)
    weighted_low = outs[0]
    parts = dict(zip(pieces, outs[1:]))
    whole = (0, owned)
    weighted_other = swap(weighted_low)
    from_ahead = ahead(parts[(2 * across, *whole)])
    from_behind = behind(parts[(0, *whole)])

    def merge(dtype, here, *arrays):
        final = len(arrays) > 2
        return pl.pallas_call(
            functools.partial(merge_kernel, closed),
            name="merge",
            out_shape=shape(here.shape, dtype),
            in_specs=vmem(1 + len(arrays)),
            out_specs=pl.BlockSpec(memory_space=pl.ANY if final else VMEM),
            scratch_shapes=[
                VMEM(here.shape if final else (1, 8, 128), f32),
                pltpu.SemaphoreType.DMA((here.shape[0],)),
            ],
            compiler_params=params(4),
            cost_estimate=cost(0.5),
        )(here, *arrays)

    come = []
    for d in range(1, across):
        for cut in cuts:
            merged = merge(
                low, parts[(across + d, *cut)], ahead(parts[(2 * across + d, *cut)]), behind(parts[(d, *cut)])
            )
            come.append(sent(merged, "patch", d))
    score = pl.pallas_call(
        score_kernel,
        name="score",
        out_shape=shape((tiles, size, cols), f32),
        in_specs=vmem(5),
        out_specs=vmem(1)[0],
        compiler_params=params(4),
        cost_estimate=cost(5),
    )(weighted_low, weighted_other, prow, pcol, norm)

    score, come = lax.optimization_barrier((score, come))
    total = merge(f32, parts[(across, *whole)], from_ahead, from_behind, *come)
    return (total.reshape(1, owned, size, cols), score.reshape(exposures.shape))


def solution(mesh):
    assert mesh.shape["band"] == 2
    in_specs = (
        P(("groups", "exp"), "patch", None, "band"),
        P(("groups", "exp"), "patch", None, None, "band"),
        P(("groups", "exp"), "patch", None, None, "band"),
        P(("groups", "exp"), "patch", None, None),
        P(("groups", "exp"), "patch", None, None),
        P(("groups", "exp"), "patch", None),
        P(("groups", "exp"), "patch"),
    )
    out_specs = (
        P(("groups", "exp"), "patch", None, "band"),
        P(("groups", "exp"), "patch", None, None, "band"),
    )

    def step(*args):
        return on_device(*args)

    step = jax.shard_map(step, mesh=mesh, in_specs=in_specs, out_specs=out_specs, check_vma=False)
    return step
```

```python
import functools

import jax
import jax.numpy as jnp
import numpy as np
from jax import lax
from jax.experimental import pallas as pl
from jax.experimental.pallas import tpu as pltpu
from jax.sharding import PartitionSpec as P


HW = 10
PW = 7

sigmas = (0.75, 1.5, 3.0)
degrees = (4, 2, 2)


VMEM = pltpu.VMEM
SMEM = pltpu.SMEM


def neighbours(groups, rows):
    if groups % 2 or rows < 2:
        line = [(g * rows + i, g * rows + i + 1) for g in range(groups) for i in range(rows - 1)]
        return line, [(j, i) for i, j in line], False
    ring = []
    for g in range(0, groups, 2):
        loop = [g * rows + i for i in range(rows)] + [(g + 1) * rows + i for i in reversed(range(rows))]
        ring += list(zip(loop, loop[1:] + loop[:1]))
    return ring, [(j, i) for i, j in ring], True


def fetched(block, axis, distance):
    devices = lax.axis_size(axis)
    return lax.ppermute(block, axis, [((i + distance) % devices, i) for i in range(devices)])


def sent(block, axis, distance):
    devices = lax.axis_size(axis)
    return lax.ppermute(block, axis, [(i, (i + distance) % devices) for i in range(devices)])


def basis_terms():
    terms = []
    offset = 0
    for group in range(3):
        for first in range(degrees[group] + 1):
            for second in range(degrees[group] + 1 - first):
                terms.append((group, first, second, offset + first))
        offset = offset + degrees[group] + 1
    return terms


def norm_of(sigma, power, reach):
    grid = np.arange(-reach, reach + 1).astype(np.float64)
    base = np.exp(-grid * grid / (2.0 * sigma * sigma)) * (grid / reach) ** power
    return float(1.0 / np.sqrt(np.sum(base * base)))


def profiles_of(offset, reach):
    spot = offset.astype(jnp.float32)
    inside = jnp.abs(offset) <= reach
    tables = []
    for group in range(3):
        base = jnp.where(inside, jnp.exp(spot * spot * (-0.5 / sigmas[group] ** 2)), 0.0)
        for power in range(degrees[group] + 1):
            tables.append(base * norm_of(sigmas[group], power, reach))
            base = base * (spot / reach)
    return tables


def taps_kernel(coeff_ref, band_ref, taps_ref, edge_ref):
    tiles, held, cols = taps_ref.shape
    slots = coeff_ref.shape[2]
    group = cols // tiles
    reach = HW
    terms = basis_terms()
    lane = lax.broadcasted_iota(jnp.int32, (1, cols), 1)
    ring = profiles_of(jnp.where(lane < cols // 2, lane, lane - cols), reach)
    spread = profiles_of(lax.broadcasted_iota(jnp.int32, (held, cols), 0) - reach, reach)
    spread = [table.astype(jnp.bfloat16).astype(jnp.float32) for table in spread]
    starts = [0]
    for degree in degrees:
        starts.append(starts[-1] + degree + 1)
    across = lax.broadcasted_iota(jnp.int32, (cols, cols), 1)
    down = lax.broadcasted_iota(jnp.int32, (cols, cols), 0)
    near = jnp.abs(across - down) <= reach
    same = (across // group) == (down // group)
    count = 2 * reach + 1
    turn = jnp.where(lax.axis_index("band") == 0, group, cols - group)

    def one(t, carry):
        taps = jnp.zeros(taps_ref.shape[1:], jnp.float32)
        for p in range(len(spread)):
            vec = jnp.zeros((1, cols), jnp.float32)
            for k, term in enumerate(terms):
                if term[3] == p:
                    vec = vec + coeff_ref[0, t // slots, t % slots, k] * ring[starts[term[0]] + term[2]]
            vec = vec.astype(jnp.bfloat16).astype(jnp.float32)
            taps = taps + spread[p] * vec
        taps_ref[t] = taps
        edge_ref[t] = pltpu.roll(taps, turn, 1)
        band_ref[t, 0:cols, :] = jnp.zeros((cols, cols), jnp.bfloat16)
        band_ref[t, (count + 1) * cols :, :] = jnp.zeros((cols, cols), jnp.bfloat16)
        for u in range(count):
            full = jnp.broadcast_to(taps_ref[t, u : u + 1, :], (cols, cols))
            full = pltpu.roll(full, 0, 1, stride=1, stride_axis=0)
            full = jnp.where(near, full, 0.0).astype(jnp.bfloat16)
            band_ref[t, (count - u) * cols : (count - u + 1) * cols, :] = full
        return carry

    lax.fori_loop(0, tiles, one, 0, unroll=tiles)
    band_ref[tiles, 0:cols, :] = jnp.zeros((cols, cols), jnp.bfloat16)
    band_ref[tiles, (count + 1) * cols :, :] = jnp.zeros((cols, cols), jnp.bfloat16)
    for u in range(count):
        full = jnp.concatenate(
            [jnp.broadcast_to(edge_ref[t, u : u + 1, :], (group, cols)) for t in range(tiles)], axis=0
        )
        full = pltpu.roll(full, 0, 1, stride=1, stride_axis=0)
        full = jnp.where(same, full, 0.0).astype(jnp.bfloat16)
        band_ref[tiles, (count - u) * cols : (count - u + 1) * cols, :] = full


def alive(live_ref, t, slots):
    return jnp.where(t % slots < live_ref[0, t // slots], 1.0, 0.0)


def norms_kernel(width_ref, live_ref, own_ref, other_ref,
                 norm_ref, prow_ref, pcol_ref, dist_ref, near_ref):
    tiles, size, cols = own_ref.shape
    wide = 2 * cols
    rows = lax.broadcasted_iota(jnp.int32, (size, size), 0)
    across = lax.broadcasted_iota(jnp.int32, (size, size), 1)
    gap = rows - across
    dist_ref[...] = (gap * gap).astype(jnp.float32)
    inner = lax.broadcasted_iota(jnp.int32, (wide, cols), 0)
    outer = lax.broadcasted_iota(jnp.int32, (wide, cols), 1)
    ring = jnp.abs(inner - outer)
    ring = jnp.minimum(ring, wide - ring)
    near_ref[...] = (ring * ring).astype(jnp.float32)
    lane = lax.broadcasted_iota(jnp.int32, (size, cols), 1)
    keep = (lane >= cols // 2) == (lax.axis_index("band") == 1)
    slots = width_ref.shape[3]
    limit = float(PW * PW)
    spot = lax.broadcasted_iota(jnp.int32, (8, 128), 1)
    spot_low = spot.astype(jnp.float32) - PW

    def table(width, square):
        rate = -0.5 / (width * width)
        base = jnp.where(spot <= 2 * PW, jnp.exp(spot_low * spot_low * rate), 0.0)
        scale = 1.0 / jnp.sum(base[0:1], axis=1, keepdims=True)
        return jnp.where(square <= limit, jnp.exp(square * rate[0:1, 0:1]) * scale, 0.0)

    def one(t, carry):
        inv_own = 1.0 / own_ref[t]
        inv_other = jnp.where(keep, 1.0 / other_ref[t], 0.0)
        inv_low = jnp.concatenate([inv_own, inv_other], axis=1).astype(jnp.bfloat16)
        prow = table(jnp.full((8, 128), width_ref[0, t // slots, 0, t % slots], jnp.float32), dist_ref[...])
        prow_ref[t] = prow.astype(jnp.bfloat16)
        qrow = (prow * prow).astype(jnp.bfloat16)
        pcol = table(jnp.full((8, 128), width_ref[0, t // slots, 1, t % slots], jnp.float32), near_ref[...])
        pcol_ref[t] = pcol.astype(jnp.bfloat16)
        qcol = (pcol * pcol).astype(jnp.bfloat16)
        denom = jnp.dot(qrow, inv_low, preferred_element_type=jnp.float32).astype(jnp.bfloat16)
        denom = jnp.dot(denom, qcol, preferred_element_type=jnp.float32)
        norm_ref[t] = alive(live_ref, t, slots) / jnp.sqrt(denom)
        return carry

    lax.fori_loop(0, tiles, one, 0, unroll=tiles)


PAD = 16


def place(ids_ref, t, owned, closed):
    slots = ids_ref.shape[2]
    row = lax.axis_index("exp")
    rows = lax.axis_size("exp")
    columns = lax.axis_size("patch")
    flip = lax.rem(lax.axis_index("groups"), 2) if closed else 0
    name = ids_ref[0, t // slots, t % slots]
    step = name // (owned * columns)
    column = name - step * (owned * columns)
    owner = column // owned
    shift = lax.rem(owner - lax.axis_index("patch") + columns, columns)
    inside = (row + step >= 1) & (row + step <= rows)
    step = jnp.where(flip == 0, step, 2 - step)
    return step * columns + shift, column - owner * owned, jnp.where(inside, 1.0, 0.0)


def clear_ends(padded_ref):
    cols = padded_ref.shape[2]
    for n in range(padded_ref.shape[0]):
        padded_ref[n, 0:PAD, :] = jnp.zeros((PAD, cols), jnp.float32)
        padded_ref[n, -PAD:, :] = jnp.zeros((PAD, cols), jnp.float32)


def build(padded_ref, lhs_ref, n):
    pairs = lhs_ref.shape[1]
    cols = padded_ref.shape[2]
    for r in range(2 * HW + 2):
        lhs_ref[n, :, r * cols : (r + 1) * cols] = padded_ref[
            n, pl.ds(PAD - HW + r, pairs, stride=2), :
        ].astype(jnp.bfloat16)


def spread(lhs_ref, band_ref, n, which):
    cols = band_ref.shape[2]
    count = 2 * HW + 2
    weights = jnp.concatenate(
        [band_ref[which, cols:, :], band_ref[which, : count * cols, :]], axis=1
    )
    return jnp.dot(lhs_ref[n], weights, preferred_element_type=jnp.float32)


def multiply_kernel(members, closed, carried, ids_ref, *refs):
    blocks = refs[: len(members)]
    band_ref = refs[len(members)]
    conv_ref, padded_ref, lhs_ref, list_ref = refs[len(members) + 1 + carried :]
    tiles, size, cols = conv_ref.shape
    owned = blocks[0].shape[0]
    side, pairs, _ = lhs_ref.shape
    clear_ends(padded_ref)

    count = 0
    for t in range(tiles):
        part, _, _ = place(ids_ref, t, owned, closed)
        here = functools.reduce(lambda a, b: a | b, [part == b for b in members])

        @pl.when(here)
        def _(t=t, count=count):
            list_ref[count] = t

        count = count + jnp.where(here, 1, 0)

    def some(i, carry):
        names = [list_ref[jnp.minimum(i * side + n, count - 1)] for n in range(side)]
        for n, t in enumerate(names):
            part, slot, _ = place(ids_ref, t, owned, closed)
            for b, ref in zip(members, blocks):
                @pl.when(part == b)
                def _(n=n, ref=ref, slot=slot):
                    padded_ref[n, PAD : PAD + size, :] = ref[slot].astype(jnp.float32)
        for n in range(side):
            build(padded_ref, lhs_ref, n)
        both = [spread(lhs_ref, band_ref, n, t) for n, t in enumerate(names)]
        for n, t in enumerate(names):
            for s in range(2):
                conv_ref[t, pl.ds(s, pairs, stride=2), :] = both[n][:, s * cols : (s + 1) * cols]
        return carry

    lax.fori_loop(0, (count + side - 1) // side, some, 0)


def convolve_kernel(blocks, closed, pieces, ids_ref, live_ref, *refs):
    other_blocks = refs[:blocks]
    (conv_ref, band_ref, exp_ref, var_ref, low_ref) = refs[blocks : blocks + 5]
    out_refs = refs[blocks + 5 : blocks + 5 + len(pieces)]
    tile_ref, padded_ref, lhs_ref, edge_ref, acc_ref = refs[blocks + 5 + len(pieces) :]
    tiles, size, cols = tile_ref.shape
    owned = other_blocks[0].shape[0]
    slots = ids_ref.shape[2]
    group = cols // tiles
    pairs = size // 2
    core = lax.axis_index("band")

    for t in range(tiles):
        part, slot, _ = place(ids_ref, t, owned, closed)
        for b in range(blocks):
            @pl.when(part == b)
            def _(t=t, b=b, slot=slot):
                tile_ref[t] = other_blocks[b][slot]

    acc_ref[...] = jnp.zeros_like(acc_ref)
    clear_ends(padded_ref)
    lane = lax.broadcasted_iota(jnp.int32, (1, cols), 1)
    start = jnp.where(core == 0, 0, cols - group)
    target = cols - group - start
    strip = jnp.zeros((size, cols), jnp.float32)
    for t in range(tiles):
        moved = pltpu.roll(tile_ref[t].astype(jnp.float32), lax.rem(t * group - start + cols, cols), 1)
        strip = jnp.where(lane // group == t, moved, strip)
    padded_ref[0, PAD : PAD + size, :] = strip
    build(padded_ref, lhs_ref, 0)
    both = spread(lhs_ref, band_ref, 0, tiles)
    for s in range(2):
        edge_ref[pl.ds(s, pairs, stride=2), :] = both[:, s * cols : (s + 1) * cols]

    def one(t, carry):
        edge = pltpu.roll(edge_ref[...], lax.rem(target - t * group + cols, cols), 1)
        edge = jnp.where((lane >= target) & (lane < target + group), edge, 0.0)
        part, slot, present = place(ids_ref, t, owned, closed)
        convolved = (conv_ref[t] + edge) * present
        own = (exp_ref[t].astype(jnp.float32) - convolved) * (1.0 / var_ref[t])
        low_ref[t] = own.astype(jnp.bfloat16)
        acc_ref[part * owned + slot] += alive(live_ref, t, slots) * own
        return carry

    lax.fori_loop(0, tiles, one, 0, unroll=2)
    for ref, (b, begin, end) in zip(out_refs, pieces):
        ref[...] = acc_ref[b * owned + begin : b * owned + end].astype(ref.dtype)


def score_kernel(low_ref, other_ref, prow_ref, pcol_ref, norm_ref, score_ref):
    tiles, size, cols = low_ref.shape
    lane = lax.broadcasted_iota(jnp.int32, (size, cols), 1)
    keep = (lane >= cols // 2) == (lax.axis_index("band") == 1)

    def one(t, carry):
        other = jnp.where(keep, other_ref[t].astype(jnp.float32), 0.0).astype(jnp.bfloat16)
        full = jnp.concatenate([low_ref[t], other], axis=1)
        numer = jnp.dot(prow_ref[t], full, preferred_element_type=jnp.float32)
        numer = numer.astype(jnp.bfloat16)
        numer = jnp.dot(numer, pcol_ref[t], preferred_element_type=jnp.float32)
        score_ref[t] = numer * norm_ref[t]
        return carry

    lax.fori_loop(0, tiles, one, 0, unroll=tiles)


def merge_kernel(closed, here_ref, first_ref, last_ref, *refs):
    row = lax.axis_index("exp")
    rows = lax.axis_size("exp")
    flip = lax.rem(lax.axis_index("groups"), 2) if closed else 0
    has_first = jnp.where(flip == 0, row > 0, row < rows - 1)
    has_last = jnp.where(flip == 0, row < rows - 1, row > 0)
    out_ref, made_ref, sem = refs[-3:]
    come = refs[:-3]
    owned = here_ref.shape[0]
    cuts = halves(owned)
    moves = []
    for patch in range(owned):
        total = here_ref[patch].astype(jnp.float32)
        total = total + jnp.where(has_first, first_ref[patch].astype(jnp.float32), 0.0)
        total = total + jnp.where(has_last, last_ref[patch].astype(jnp.float32), 0.0)
        for n, ref in enumerate(come):
            begin, end = cuts[n % len(cuts)]
            if begin <= patch < end:
                total = total + ref[patch - begin].astype(jnp.float32)
        if not come:
            out_ref[patch] = total.astype(out_ref.dtype)
        else:
            made_ref[patch] = total
            moves.append(pltpu.make_async_copy(made_ref.at[patch], out_ref.at[patch], sem.at[patch]))
            moves[-1].start()
    for move in moves:
        move.wait()


def halves(count):
    return [(0, count // 2), (count // 2, count)] if count % 2 == 0 else [(0, count)]


def shape(dims, dtype):
    return jax.ShapeDtypeStruct(dims, dtype)


def vmem(count):
    return [pl.BlockSpec(memory_space=VMEM)] * count


def smem(count):
    return [pl.BlockSpec(memory_space=SMEM)] * count


def params(mib):
    return pltpu.CompilerParams(vmem_limit_bytes=mib << 20)


def cost(micros):
    return pl.CostEstimate(flops=int(micros * 1e9), bytes_accessed=int(micros * 3e6), transcendentals=0)


def on_device(templates, exposures, variance, coefficients, psf_width, patch_ids, live_count):
    size = templates.shape[2]
    cols = templates.shape[3]
    owned = templates.shape[1]
    across = lax.axis_size("patch")
    blocks = 3 * across
    low = jnp.bfloat16
    f32 = jnp.float32

    own = templates.reshape(owned, size, cols)
    exp_flat = exposures.reshape(-1, size, cols)
    var_flat = variance.reshape(-1, size, cols)
    tiles = exp_flat.shape[0]
    assert cols % tiles == 0 and cols // tiles >= HW and size % 32 == 0
    swap = functools.partial(sent, axis="band", distance=1)

    forth, back, closed = neighbours(lax.axis_size("groups"), lax.axis_size("exp"))
    ahead = lambda block: lax.ppermute(block, ("groups", "exp"), forth)
    behind = lambda block: lax.ppermute(block, ("groups", "exp"), back)
    row = [own] + [fetched(own, "patch", d) for d in range(1, across)]
    firsts = [ahead(own)]
    lasts = [behind(own)]
    var_other = swap(var_flat)

    count = 2 * HW + 1
    held = -(-count // 8) * 8
    band = pl.pallas_call(
        taps_kernel,
        name="taps",
        out_shape=shape((tiles + 1, (count + 2) * cols, cols), low),
        in_specs=smem(1),
        out_specs=vmem(1)[0],
        scratch_shapes=[VMEM((tiles, held, cols), f32), VMEM((tiles, held, cols), f32)],
        compiler_params=params(4),
        cost_estimate=cost(3),
    )(coefficients)
    band, row = lax.optimization_barrier((band, row))
    firsts += [ahead(row[d]) for d in range(1, across)]
    lasts += [behind(row[d]) for d in range(1, across)]

    norm, prow, pcol = pl.pallas_call(
        norms_kernel,
        name="norms",
        out_shape=(
            shape((tiles, size, cols), f32),
            shape((tiles, size, size), low),
            shape((tiles, 2 * cols, cols), low),
        ),
        in_specs=smem(2) + vmem(2),
        out_specs=tuple(vmem(3)),
        scratch_shapes=[VMEM((size, size), f32), VMEM((2 * cols, cols), f32)],
        compiler_params=params(6),
        cost_estimate=cost(5),
    )(jnp.swapaxes(psf_width, 2, 3), live_count, var_flat, var_other)
    side = 2 if tiles % 2 == 0 else 1

    def multiply(members, sources, *carried):
        return pl.pallas_call(
            functools.partial(multiply_kernel, members, closed, len(carried)),
            name="multiply",
            out_shape=shape((tiles, size, cols), f32),
            in_specs=smem(1) + vmem(len(sources) + 1 + len(carried)),
            out_specs=vmem(1)[0],
            input_output_aliases={len(sources) + 2: 0} if carried else {},
            scratch_shapes=[
                VMEM((side, size + 2 * PAD, cols), f32),
                VMEM((side, size // 2, (count + 1) * cols), low),
                SMEM((tiles,), jnp.int32),
            ],
            compiler_params=params(8),
            cost_estimate=cost(3),
        )(patch_ids, *sources, band, *carried)

    soon = [0] + list(range(across, 2 * across)) + [2 * across]
    conv = multiply(soon, [firsts[0]] + row + [lasts[0]])
    norm, conv, firsts[1:], lasts[1:] = lax.optimization_barrier(
        (norm, conv, firsts[1:], lasts[1:])
    )
    early = [swap(b) for b in [firsts[0]] + row + [lasts[0]]]
    later = [b for b in range(blocks) if b not in soon]
    if later:
        conv = multiply(later, firsts[1:] + lasts[1:], conv)
    window_other = early[:1] + [swap(b) for b in firsts[1:]] + early[1:-1]
    window_other = window_other + early[-1:] + [swap(b) for b in lasts[1:]]

    cuts = halves(owned)
    pieces = [(b, 0, owned) for b in (0, across, 2 * across)]
    pieces += [(n * across + d, *cut) for d in range(1, across) for cut in cuts for n in range(3)]
    outs = pl.pallas_call(
        functools.partial(convolve_kernel, blocks, closed, pieces),
        name="convolve",
        out_shape=tuple(
            [shape((tiles, size, cols), low)]
            + [shape((e - a, size, cols), f32 if b == across else low) for b, a, e in pieces]
        ),
        in_specs=smem(2) + vmem(blocks + 4),
        out_specs=tuple(vmem(1 + len(pieces))),
        scratch_shapes=[
            VMEM((tiles, size, cols), low),
            VMEM((1, size + 2 * PAD, cols), f32),
            VMEM((1, size // 2, (count + 1) * cols), low),
            VMEM((size, cols), f32),
            VMEM((blocks * owned, size, cols), f32),
        ],
        compiler_params=params(12),
        cost_estimate=cost(5),
    )(patch_ids, live_count, *window_other, conv, band, exp_flat, var_flat)
    weighted_low = outs[0]
    parts = dict(zip(pieces, outs[1:]))
    whole = (0, owned)
    weighted_other = swap(weighted_low)
    from_ahead = ahead(parts[(2 * across, *whole)])
    from_behind = behind(parts[(0, *whole)])

    def merge(dtype, here, *arrays):
        final = len(arrays) > 2
        return pl.pallas_call(
            functools.partial(merge_kernel, closed),
            name="merge",
            out_shape=shape(here.shape, dtype),
            in_specs=vmem(1 + len(arrays)),
            out_specs=pl.BlockSpec(memory_space=pl.ANY if final else VMEM),
            scratch_shapes=[
                VMEM(here.shape if final else (1, 8, 128), f32),
                pltpu.SemaphoreType.DMA((here.shape[0],)),
            ],
            compiler_params=params(4),
            cost_estimate=cost(0.5),
        )(here, *arrays)

    come = []
    for d in range(1, across):
        for cut in cuts:
            merged = merge(
                low,
                parts[(across + d, *cut)],
                ahead(parts[(2 * across + d, *cut)]),
                behind(parts[(d, *cut)]),
            )
            come.append(sent(merged, "patch", d))
    score = pl.pallas_call(
        score_kernel,
        name="score",
        out_shape=shape((tiles, size, cols), f32),
        in_specs=vmem(5),
        out_specs=vmem(1)[0],
        compiler_params=params(4),
        cost_estimate=cost(5),
    )(weighted_low, weighted_other, prow, pcol, norm)

    score, come = lax.optimization_barrier((score, come))
    total = merge(f32, parts[(across, *whole)], from_ahead, from_behind, *come)
    return (total.reshape(1, owned, size, cols), score.reshape(exposures.shape))


def solution(mesh):
    assert mesh.shape["band"] == 2
    in_specs = (
        P(("groups", "exp"), "patch", None, "band"),
        P(("groups", "exp"), "patch", None, None, "band"),
        P(("groups", "exp"), "patch", None, None, "band"),
        P(("groups", "exp"), "patch", None, None),
        P(("groups", "exp"), "patch", None, None),
        P(("groups", "exp"), "patch", None),
        P(("groups", "exp"), "patch"),
    )
    out_specs = (
        P(("groups", "exp"), "patch", None, "band"),
        P(("groups", "exp"), "patch", None, None, "band"),
    )

    def step(*args):
        return on_device(*args)

    step = jax.shard_map(step, mesh=mesh, in_specs=in_specs, out_specs=out_specs, check_vma=False)
    return step
```

```python
import functools

import jax
import jax.numpy as jnp
import numpy as np
from jax import lax
from jax.experimental import pallas as pl
from jax.experimental.pallas import tpu as pltpu
from jax.sharding import PartitionSpec as P


HW = 10
PW = 7

sigmas = (0.75, 1.5, 3.0)
degrees = (4, 2, 2)


VMEM = pltpu.VMEM
SMEM = pltpu.SMEM


def neighbours(groups, rows):
    if groups % 2 or rows < 2:
        line = [(g * rows + i, g * rows + i + 1) for g in range(groups) for i in range(rows - 1)]
        return line, [(j, i) for i, j in line], False
    ring = []
    for g in range(0, groups, 2):
        loop = [g * rows + i for i in range(rows)] + [(g + 1) * rows + i for i in reversed(range(rows))]
        ring += list(zip(loop, loop[1:] + loop[:1]))
    return ring, [(j, i) for i, j in ring], True


def fetched(block, axis, distance):
    devices = lax.axis_size(axis)
    return lax.ppermute(block, axis, [((i + distance) % devices, i) for i in range(devices)])


def sent(block, axis, distance):
    devices = lax.axis_size(axis)
    return lax.ppermute(block, axis, [(i, (i + distance) % devices) for i in range(devices)])


def basis_terms():
    terms = []
    offset = 0
    for group in range(3):
        for first in range(degrees[group] + 1):
            for second in range(degrees[group] + 1 - first):
                terms.append((group, first, second, offset + first))
        offset = offset + degrees[group] + 1
    return terms


def norm_of(sigma, power, reach):
    grid = np.arange(-reach, reach + 1).astype(np.float64)
    base = np.exp(-grid * grid / (2.0 * sigma * sigma)) * (grid / reach) ** power
    return float(1.0 / np.sqrt(np.sum(base * base)))


def profiles_of(offset, reach):
    spot = offset.astype(jnp.float32)
    inside = jnp.abs(offset) <= reach
    tables = []
    for group in range(3):
        base = jnp.where(inside, jnp.exp(spot * spot * (-0.5 / sigmas[group] ** 2)), 0.0)
        for power in range(degrees[group] + 1):
            tables.append(base * norm_of(sigmas[group], power, reach))
            base = base * (spot / reach)
    return tables


def taps_kernel(coeff_ref, band_ref, taps_ref, edge_ref):
    tiles, held, cols = taps_ref.shape
    slots = coeff_ref.shape[2]
    group = cols // tiles
    reach = HW
    terms = basis_terms()
    lane = lax.broadcasted_iota(jnp.int32, (1, cols), 1)
    ring = profiles_of(jnp.where(lane < cols // 2, lane, lane - cols), reach)
    spread = profiles_of(lax.broadcasted_iota(jnp.int32, (held, cols), 0) - reach, reach)
    spread = [table.astype(jnp.bfloat16).astype(jnp.float32) for table in spread]
    starts = [0]
    for degree in degrees:
        starts.append(starts[-1] + degree + 1)
    across = lax.broadcasted_iota(jnp.int32, (cols, cols), 1)
    down = lax.broadcasted_iota(jnp.int32, (cols, cols), 0)
    near = jnp.abs(across - down) <= reach
    same = (across // group) == (down // group)
    count = 2 * reach + 1
    turn = jnp.where(lax.axis_index("band") == 0, group, cols - group)

    def one(t, carry):
        taps = jnp.zeros(taps_ref.shape[1:], jnp.float32)
        for p in range(len(spread)):
            vec = jnp.zeros((1, cols), jnp.float32)
            for k, term in enumerate(terms):
                if term[3] == p:
                    vec = vec + coeff_ref[0, t // slots, t % slots, k] * ring[starts[term[0]] + term[2]]
            vec = vec.astype(jnp.bfloat16).astype(jnp.float32)
            taps = taps + spread[p] * vec
        taps_ref[t] = taps
        edge_ref[t] = pltpu.roll(taps, turn, 1)
        band_ref[t, 0:cols, :] = jnp.zeros((cols, cols), jnp.bfloat16)
        band_ref[t, (count + 1) * cols :, :] = jnp.zeros((cols, cols), jnp.bfloat16)
        for u in range(count):
            full = jnp.broadcast_to(taps_ref[t, u : u + 1, :], (cols, cols))
            full = pltpu.roll(full, 0, 1, stride=1, stride_axis=0)
            full = jnp.where(near, full, 0.0).astype(jnp.bfloat16)
            band_ref[t, (count - u) * cols : (count - u + 1) * cols, :] = full
        return carry

    lax.fori_loop(0, tiles, one, 0, unroll=tiles)
    band_ref[tiles, 0:cols, :] = jnp.zeros((cols, cols), jnp.bfloat16)
    band_ref[tiles, (count + 1) * cols :, :] = jnp.zeros((cols, cols), jnp.bfloat16)
    for u in range(count):
        full = jnp.concatenate(
            [jnp.broadcast_to(edge_ref[t, u : u + 1, :], (group, cols)) for t in range(tiles)], axis=0
        )
        full = pltpu.roll(full, 0, 1, stride=1, stride_axis=0)
        full = jnp.where(same, full, 0.0).astype(jnp.bfloat16)
        band_ref[tiles, (count - u) * cols : (count - u + 1) * cols, :] = full


def alive(live_ref, t, slots):
    return jnp.where(t % slots < live_ref[0, t // slots], 1.0, 0.0)


def norms_kernel(width_ref, live_ref, own_ref, other_ref, norm_ref, inv_ref, prow_ref, pcol_ref):
    tiles, size, cols = own_ref.shape
    blocks = size // cols
    lane = lax.broadcasted_iota(jnp.int32, (size, cols), 1)
    keep = (lane >= cols // 2) == (lax.axis_index("band") == 1)
    slots = width_ref.shape[3]
    down = lax.broadcasted_iota(jnp.int32, (cols, cols), 0)
    across = lax.broadcasted_iota(jnp.int32, (cols, cols), 1)
    gaps = (down - across, (down + cols - across)[:8], (down - cols - across)[-8:])
    squares = [(gap * gap).astype(jnp.float32) for gap in gaps]
    spot = lax.broadcasted_iota(jnp.int32, (8, 128), 1)
    spot_low = spot.astype(jnp.float32) - PW

    def table(width):
        width = jnp.full((8, 128), width, jnp.float32)
        rate = -0.5 / (width * width)
        base = jnp.where(spot <= 2 * PW, jnp.exp(spot_low * spot_low * rate), 0.0)
        scale = 1.0 / jnp.sum(base[0:1], axis=1, keepdims=True)
        return [
            jnp.where(square <= float(PW * PW), jnp.exp(square * rate[0:1, 0:1]) * scale, 0.0)
            for square in squares
        ]

    def gap(rows):
        return jnp.zeros((rows, cols), jnp.float32)

    def row_matrix(main, low, high):
        up = jnp.concatenate([gap(cols - 8), high], axis=0)
        under = jnp.concatenate([low, gap(cols - 8)], axis=0)
        choice = {0: main, 1: up, -1: under}
        return jnp.concatenate(
            [
                jnp.concatenate([choice.get(b - a, gap(cols)) for b in range(blocks)], axis=1)
                for a in range(blocks)
            ],
            axis=0,
        ).astype(jnp.bfloat16)

    def column_matrix(main, low, high):
        return jnp.concatenate([main, low, gap(cols - 16), high], axis=0).astype(jnp.bfloat16)

    def one(t, carry):
        inv_own = 1.0 / own_ref[t]
        inv_ref[t] = inv_own
        inv_other = jnp.where(keep, 1.0 / other_ref[t], 0.0)
        inv_low = jnp.concatenate([inv_own, inv_other], axis=1).astype(jnp.bfloat16)
        prow = table(width_ref[0, t // slots, 0, t % slots])
        pcol = table(width_ref[0, t // slots, 1, t % slots])
        prow_ref[t] = row_matrix(*prow)
        pcol_ref[t] = column_matrix(*pcol)
        qrow = row_matrix(*[value * value for value in prow])
        qcol = column_matrix(*[value * value for value in pcol])
        denom = jnp.dot(qrow, inv_low, preferred_element_type=jnp.float32).astype(jnp.bfloat16)
        denom = jnp.dot(denom, qcol, preferred_element_type=jnp.float32)
        norm_ref[t] = alive(live_ref, t, slots) / jnp.sqrt(denom)
        return carry

    lax.fori_loop(0, tiles, one, 0, unroll=tiles)


PAD = 16


def place(ids_ref, t, owned, closed):
    slots = ids_ref.shape[2]
    row = lax.axis_index("exp")
    rows = lax.axis_size("exp")
    columns = lax.axis_size("patch")
    flip = lax.rem(lax.axis_index("groups"), 2) if closed else 0
    name = ids_ref[0, t // slots, t % slots]
    step = name // (owned * columns)
    column = name - step * (owned * columns)
    owner = column // owned
    shift = lax.rem(owner - lax.axis_index("patch") + columns, columns)
    inside = (row + step >= 1) & (row + step <= rows)
    step = jnp.where(flip == 0, step, 2 - step)
    return step * columns + shift, column - owner * owned, jnp.where(inside, 1.0, 0.0)


def clear_ends(padded_ref):
    cols = padded_ref.shape[2]
    for n in range(padded_ref.shape[0]):
        padded_ref[n, 0:PAD, :] = jnp.zeros((PAD, cols), jnp.float32)
        padded_ref[n, -PAD:, :] = jnp.zeros((PAD, cols), jnp.float32)


def build(padded_ref, lhs_ref, n):
    pairs = lhs_ref.shape[1]
    cols = padded_ref.shape[2]
    for r in range(2 * HW + 2):
        lhs_ref[n, :, r * cols : (r + 1) * cols] = padded_ref[
            n, pl.ds(PAD - HW + r, pairs, stride=2), :
        ].astype(jnp.bfloat16)


def spread(lhs_ref, band_ref, n, which):
    cols = band_ref.shape[2]
    count = 2 * HW + 2
    weights = jnp.concatenate(
        [band_ref[which, cols:, :], band_ref[which, : count * cols, :]], axis=1
    )
    return jnp.dot(lhs_ref[n], weights, preferred_element_type=jnp.float32)


def multiply_kernel(members, closed, carried, ids_ref, *refs):
    blocks = refs[: len(members)]
    band_ref = refs[len(members)]
    conv_ref, padded_ref, lhs_ref, list_ref = refs[len(members) + 1 + carried :]
    tiles, size, cols = conv_ref.shape
    owned = blocks[0].shape[0]
    side, pairs, _ = lhs_ref.shape
    clear_ends(padded_ref)

    count = 0
    for t in range(tiles):
        part, _, _ = place(ids_ref, t, owned, closed)
        here = functools.reduce(lambda a, b: a | b, [part == b for b in members])

        @pl.when(here)
        def _(t=t, count=count):
            list_ref[count] = t

        count = count + jnp.where(here, 1, 0)

    def some(i, carry):
        names = [list_ref[jnp.minimum(i * side + n, count - 1)] for n in range(side)]
        for n, t in enumerate(names):
            part, slot, _ = place(ids_ref, t, owned, closed)
            for b, ref in zip(members, blocks):
                @pl.when(part == b)
                def _(n=n, ref=ref, slot=slot):
                    padded_ref[n, PAD : PAD + size, :] = ref[slot].astype(jnp.float32)
        for n in range(side):
            build(padded_ref, lhs_ref, n)
        both = [spread(lhs_ref, band_ref, n, t) for n, t in enumerate(names)]
        for n, t in enumerate(names):
            for s in range(2):
                conv_ref[t, pl.ds(s, pairs, stride=2), :] = both[n][:, s * cols : (s + 1) * cols]
        return carry

    lax.fori_loop(0, (count + side - 1) // side, some, 0)


def convolve_kernel(blocks, closed, pieces, ids_ref, live_ref, *refs):
    other_blocks = refs[:blocks]
    (conv_ref, band_ref, exp_ref, inv_ref, low_ref) = refs[blocks : blocks + 5]
    out_refs = refs[blocks + 5 : blocks + 5 + len(pieces)]
    tile_ref, padded_ref, lhs_ref, edge_ref, acc_ref = refs[blocks + 5 + len(pieces) :]
    tiles, size, cols = tile_ref.shape
    owned = other_blocks[0].shape[0]
    slots = ids_ref.shape[2]
    group = cols // tiles
    pairs = size // 2
    core = lax.axis_index("band")

    for t in range(tiles):
        part, slot, _ = place(ids_ref, t, owned, closed)
        for b in range(blocks):
            @pl.when(part == b)
            def _(t=t, b=b, slot=slot):
                tile_ref[t] = other_blocks[b][slot]

    acc_ref[...] = jnp.zeros_like(acc_ref)
    clear_ends(padded_ref)
    lane = lax.broadcasted_iota(jnp.int32, (1, cols), 1)
    start = jnp.where(core == 0, 0, cols - group)
    target = cols - group - start
    strip = jnp.zeros((size, cols), jnp.float32)
    for t in range(tiles):
        moved = pltpu.roll(tile_ref[t].astype(jnp.float32), lax.rem(t * group - start + cols, cols), 1)
        strip = jnp.where(lane // group == t, moved, strip)
    padded_ref[0, PAD : PAD + size, :] = strip
    build(padded_ref, lhs_ref, 0)
    both = spread(lhs_ref, band_ref, 0, tiles)
    for s in range(2):
        edge_ref[pl.ds(s, pairs, stride=2), :] = both[:, s * cols : (s + 1) * cols]

    def one(t, carry):
        edge = pltpu.roll(edge_ref[...], lax.rem(target - t * group + cols, cols), 1)
        edge = jnp.where((lane >= target) & (lane < target + group), edge, 0.0)
        part, slot, present = place(ids_ref, t, owned, closed)
        convolved = (conv_ref[t] + edge) * present
        own = (exp_ref[t].astype(jnp.float32) - convolved) * inv_ref[t]
        low_ref[t] = own.astype(jnp.bfloat16)
        acc_ref[part * owned + slot] += alive(live_ref, t, slots) * own
        return carry

    lax.fori_loop(0, tiles, one, 0, unroll=8)
    for ref, (b, begin, end) in zip(out_refs, pieces):
        ref[...] = acc_ref[b * owned + begin : b * owned + end].astype(ref.dtype)


def score_kernel(low_ref, other_ref, prow_ref, pcol_ref, norm_ref, score_ref):
    tiles, size, cols = low_ref.shape
    lane = lax.broadcasted_iota(jnp.int32, (size, cols), 1)
    keep = (lane >= cols // 2) == (lax.axis_index("band") == 1)

    def one(t, carry):
        other = jnp.where(keep, other_ref[t].astype(jnp.float32), 0.0).astype(jnp.bfloat16)
        full = jnp.concatenate([low_ref[t], other], axis=1)
        numer = jnp.dot(prow_ref[t], full, preferred_element_type=jnp.float32)
        numer = numer.astype(jnp.bfloat16)
        numer = jnp.dot(numer, pcol_ref[t], preferred_element_type=jnp.float32)
        score_ref[t] = numer * norm_ref[t]
        return carry

    lax.fori_loop(0, tiles, one, 0, unroll=tiles)


def merge_kernel(closed, here_ref, first_ref, last_ref, *refs):
    row = lax.axis_index("exp")
    rows = lax.axis_size("exp")
    flip = lax.rem(lax.axis_index("groups"), 2) if closed else 0
    has_first = jnp.where(flip == 0, row > 0, row < rows - 1)
    has_last = jnp.where(flip == 0, row < rows - 1, row > 0)
    out_ref, made_ref, sem = refs[-3:]
    come = refs[:-3]
    owned = here_ref.shape[0]
    cuts = halves(owned)
    moves = []
    for patch in range(owned):
        total = here_ref[patch].astype(jnp.float32)
        total = total + jnp.where(has_first, first_ref[patch].astype(jnp.float32), 0.0)
        total = total + jnp.where(has_last, last_ref[patch].astype(jnp.float32), 0.0)
        for n, ref in enumerate(come):
            begin, end = cuts[n % len(cuts)]
            if begin <= patch < end:
                total = total + ref[patch - begin].astype(jnp.float32)
        if not come:
            out_ref[patch] = total.astype(out_ref.dtype)
        else:
            made_ref[patch] = total
            moves.append(pltpu.make_async_copy(made_ref.at[patch], out_ref.at[patch], sem.at[patch]))
            moves[-1].start()
    for move in moves:
        move.wait()


def halves(count):
    return [(0, count // 2), (count // 2, count)] if count % 2 == 0 else [(0, count)]


def shape(dims, dtype):
    return jax.ShapeDtypeStruct(dims, dtype)


def vmem(count):
    return [pl.BlockSpec(memory_space=VMEM)] * count


def smem(count):
    return [pl.BlockSpec(memory_space=SMEM)] * count


def params(mib):
    return pltpu.CompilerParams(vmem_limit_bytes=mib << 20)


def cost(micros):
    return pl.CostEstimate(flops=int(micros * 1e9), bytes_accessed=int(micros * 3e6), transcendentals=0)


def on_device(templates, exposures, variance, coefficients, psf_width, patch_ids, live_count):
    size = templates.shape[2]
    cols = templates.shape[3]
    owned = templates.shape[1]
    across = lax.axis_size("patch")
    blocks = 3 * across
    low = jnp.bfloat16
    f32 = jnp.float32

    own = templates.reshape(owned, size, cols)
    exp_flat = exposures.reshape(-1, size, cols)
    var_flat = variance.reshape(-1, size, cols)
    tiles = exp_flat.shape[0]
    assert cols % tiles == 0 and cols // tiles >= HW and size % cols == 0 and PW < 8
    swap = functools.partial(sent, axis="band", distance=1)

    forth, back, closed = neighbours(lax.axis_size("groups"), lax.axis_size("exp"))
    ahead = lambda block: lax.ppermute(block, ("groups", "exp"), forth)
    behind = lambda block: lax.ppermute(block, ("groups", "exp"), back)
    row = [own] + [fetched(own, "patch", d) for d in range(1, across)]
    firsts = [ahead(own)]
    lasts = [behind(own)]
    var_other = swap(var_flat)

    count = 2 * HW + 1
    held = -(-count // 8) * 8
    band = pl.pallas_call(
        taps_kernel,
        name="taps",
        out_shape=shape((tiles + 1, (count + 2) * cols, cols), low),
        in_specs=smem(1),
        out_specs=vmem(1)[0],
        scratch_shapes=[VMEM((tiles, held, cols), f32), VMEM((tiles, held, cols), f32)],
        compiler_params=params(4),
        cost_estimate=cost(3),
    )(coefficients)
    band, row = lax.optimization_barrier((band, row))
    firsts += [ahead(row[d]) for d in range(1, across)]
    lasts += [behind(row[d]) for d in range(1, across)]

    norm, inv, prow, pcol = pl.pallas_call(
        norms_kernel,
        name="norms",
        out_shape=(
            shape((tiles, size, cols), f32),
            shape((tiles, size, cols), f32),
            shape((tiles, size, size), low),
            shape((tiles, 2 * cols, cols), low),
        ),
        in_specs=smem(2) + vmem(2),
        out_specs=tuple(vmem(4)),
        compiler_params=params(6),
        cost_estimate=cost(5),
    )(jnp.swapaxes(psf_width, 2, 3), live_count, var_flat, var_other)
    side = 2 if tiles % 2 == 0 else 1

    def multiply(members, sources, *carried):
        return pl.pallas_call(
            functools.partial(multiply_kernel, members, closed, len(carried)),
            name="multiply",
            out_shape=shape((tiles, size, cols), f32),
            in_specs=smem(1) + vmem(len(sources) + 1 + len(carried)),
            out_specs=vmem(1)[0],
            input_output_aliases={len(sources) + 2: 0} if carried else {},
            scratch_shapes=[
                VMEM((side, size + 2 * PAD, cols), f32),
                VMEM((side, size // 2, (count + 1) * cols), low),
                SMEM((tiles,), jnp.int32),
            ],
            compiler_params=params(8),
            cost_estimate=cost(3),
        )(patch_ids, *sources, band, *carried)

    soon = [0] + list(range(across, 2 * across)) + [2 * across]
    conv = multiply(soon, [firsts[0]] + row + [lasts[0]])
    norm, conv, firsts[1:], lasts[1:] = lax.optimization_barrier(
        (norm, conv, firsts[1:], lasts[1:])
    )
    early = [swap(b) for b in [firsts[0]] + row + [lasts[0]]]
    later = [b for b in range(blocks) if b not in soon]
    if later:
        conv = multiply(later, firsts[1:] + lasts[1:], conv)
    window_other = early[:1] + [swap(b) for b in firsts[1:]] + early[1:-1]
    window_other = window_other + early[-1:] + [swap(b) for b in lasts[1:]]

    cuts = halves(owned)
    pieces = [(b, 0, owned) for b in (0, across, 2 * across)]
    pieces += [(n * across + d, *cut) for d in range(1, across) for cut in cuts for n in range(3)]
    outs = pl.pallas_call(
        functools.partial(convolve_kernel, blocks, closed, pieces),
        name="convolve",
        out_shape=tuple(
            [shape((tiles, size, cols), low)]
            + [shape((e - a, size, cols), f32 if b == across else low) for b, a, e in pieces]
        ),
        in_specs=smem(2) + vmem(blocks + 4),
        out_specs=tuple(vmem(1 + len(pieces))),
        scratch_shapes=[
            VMEM((tiles, size, cols), low),
            VMEM((1, size + 2 * PAD, cols), f32),
            VMEM((1, size // 2, (count + 1) * cols), low),
            VMEM((size, cols), f32),
            VMEM((blocks * owned, size, cols), f32),
        ],
        compiler_params=params(12),
        cost_estimate=cost(5),
    )(patch_ids, live_count, *window_other, conv, band, exp_flat, inv)
    weighted_low = outs[0]
    parts = dict(zip(pieces, outs[1:]))
    whole = (0, owned)
    weighted_other = swap(weighted_low)
    from_ahead = ahead(parts[(2 * across, *whole)])
    from_behind = behind(parts[(0, *whole)])

    def merge(dtype, here, *arrays):
        final = len(arrays) > 2
        return pl.pallas_call(
            functools.partial(merge_kernel, closed),
            name="merge",
            out_shape=shape(here.shape, dtype),
            in_specs=vmem(1 + len(arrays)),
            out_specs=pl.BlockSpec(memory_space=pl.ANY if final else VMEM),
            scratch_shapes=[
                VMEM(here.shape if final else (1, 8, 128), f32),
                pltpu.SemaphoreType.DMA((here.shape[0],)),
            ],
            compiler_params=params(4),
            cost_estimate=cost(0.5),
        )(here, *arrays)

    come = []
    for d in range(1, across):
        for cut in cuts:
            merged = merge(
                low,
                parts[(across + d, *cut)],
                ahead(parts[(2 * across + d, *cut)]),
                behind(parts[(d, *cut)]),
            )
            come.append(sent(merged, "patch", d))
    score = pl.pallas_call(
        score_kernel,
        name="score",
        out_shape=shape((tiles, size, cols), f32),
        in_specs=vmem(5),
        out_specs=vmem(1)[0],
        compiler_params=params(4),
        cost_estimate=cost(5),
    )(weighted_low, weighted_other, prow, pcol, norm)

    score, come = lax.optimization_barrier((score, come))
    total = merge(f32, parts[(across, *whole)], from_ahead, from_behind, *come)
    return (total.reshape(1, owned, size, cols), score.reshape(exposures.shape))


def solution(mesh):
    assert mesh.shape["band"] == 2
    in_specs = (
        P(("groups", "exp"), "patch", None, "band"),
        P(("groups", "exp"), "patch", None, None, "band"),
        P(("groups", "exp"), "patch", None, None, "band"),
        P(("groups", "exp"), "patch", None, None),
        P(("groups", "exp"), "patch", None, None),
        P(("groups", "exp"), "patch", None),
        P(("groups", "exp"), "patch"),
    )
    out_specs = (
        P(("groups", "exp"), "patch", None, "band"),
        P(("groups", "exp"), "patch", None, None, "band"),
    )

    def step(*args):
        return on_device(*args)

    step = jax.shard_map(step, mesh=mesh, in_specs=in_specs, out_specs=out_specs, check_vma=False)
    return step
```

```python
import functools

import jax
import jax.numpy as jnp
import numpy as np
from jax import lax
from jax.experimental import pallas as pl
from jax.experimental.pallas import tpu as pltpu
from jax.sharding import PartitionSpec as P


HW = 10
PW = 7

sigmas = (0.75, 1.5, 3.0)
degrees = (4, 2, 2)


VMEM = pltpu.VMEM
SMEM = pltpu.SMEM


def neighbours(groups, rows):
    if groups % 2 or rows < 2:
        line = [(g * rows + i, g * rows + i + 1) for g in range(groups) for i in range(rows - 1)]
        return line, [(j, i) for i, j in line], False
    ring = []
    for g in range(0, groups, 2):
        loop = [g * rows + i for i in range(rows)] + [(g + 1) * rows + i for i in reversed(range(rows))]
        ring += list(zip(loop, loop[1:] + loop[:1]))
    return ring, [(j, i) for i, j in ring], True


def fetched(block, axis, distance):
    devices = lax.axis_size(axis)
    return lax.ppermute(block, axis, [((i + distance) % devices, i) for i in range(devices)])


def sent(block, axis, distance):
    devices = lax.axis_size(axis)
    return lax.ppermute(block, axis, [(i, (i + distance) % devices) for i in range(devices)])


def basis_terms():
    terms = []
    offset = 0
    for group in range(3):
        for first in range(degrees[group] + 1):
            for second in range(degrees[group] + 1 - first):
                terms.append((group, first, second, offset + first))
        offset = offset + degrees[group] + 1
    return terms


def norm_of(sigma, power, reach):
    grid = np.arange(-reach, reach + 1).astype(np.float64)
    base = np.exp(-grid * grid / (2.0 * sigma * sigma)) * (grid / reach) ** power
    return float(1.0 / np.sqrt(np.sum(base * base)))


def profiles_of(offset, reach):
    spot = offset.astype(jnp.float32)
    inside = jnp.abs(offset) <= reach
    tables = []
    for group in range(3):
        base = jnp.where(inside, jnp.exp(spot * spot * (-0.5 / sigmas[group] ** 2)), 0.0)
        for power in range(degrees[group] + 1):
            tables.append(base * norm_of(sigmas[group], power, reach))
            base = base * (spot / reach)
    return tables


def taps_kernel(coeff_ref, band_ref, taps_ref, edge_ref):
    tiles, held, cols = taps_ref.shape
    slots = coeff_ref.shape[2]
    group = cols // tiles
    reach = HW
    terms = basis_terms()
    lane = lax.broadcasted_iota(jnp.int32, (1, cols), 1)
    ring = profiles_of(jnp.where(lane < cols // 2, lane, lane - cols), reach)
    spread = profiles_of(lax.broadcasted_iota(jnp.int32, (held, cols), 0) - reach, reach)
    spread = [table.astype(jnp.bfloat16).astype(jnp.float32) for table in spread]
    starts = [0]
    for degree in degrees:
        starts.append(starts[-1] + degree + 1)
    across = lax.broadcasted_iota(jnp.int32, (cols, cols), 1)
    down = lax.broadcasted_iota(jnp.int32, (cols, cols), 0)
    near = jnp.abs(across - down) <= reach
    same = (across // group) == (down // group)
    count = 2 * reach + 1
    turn = jnp.where(lax.axis_index("band") == 0, group, cols - group)

    def one(t, carry):
        taps = jnp.zeros(taps_ref.shape[1:], jnp.float32)
        for p in range(len(spread)):
            vec = jnp.zeros((1, cols), jnp.float32)
            for k, term in enumerate(terms):
                if term[3] == p:
                    vec = vec + coeff_ref[0, t // slots, t % slots, k] * ring[starts[term[0]] + term[2]]
            vec = vec.astype(jnp.bfloat16).astype(jnp.float32)
            taps = taps + spread[p] * vec
        taps_ref[t] = taps
        edge_ref[t] = pltpu.roll(taps, turn, 1)
        band_ref[t, 0:cols, :] = jnp.zeros((cols, cols), jnp.bfloat16)
        band_ref[t, (count + 1) * cols :, :] = jnp.zeros((cols, cols), jnp.bfloat16)
        for u in range(count):
            full = jnp.broadcast_to(taps_ref[t, u : u + 1, :], (cols, cols))
            full = pltpu.roll(full, 0, 1, stride=1, stride_axis=0)
            full = jnp.where(near, full, 0.0).astype(jnp.bfloat16)
            band_ref[t, (count - u) * cols : (count - u + 1) * cols, :] = full
        return carry

    lax.fori_loop(0, tiles, one, 0, unroll=tiles)
    band_ref[tiles, 0:cols, :] = jnp.zeros((cols, cols), jnp.bfloat16)
    band_ref[tiles, (count + 1) * cols :, :] = jnp.zeros((cols, cols), jnp.bfloat16)
    for u in range(count):
        full = jnp.concatenate(
            [jnp.broadcast_to(edge_ref[t, u : u + 1, :], (group, cols)) for t in range(tiles)], axis=0
        )
        full = pltpu.roll(full, 0, 1, stride=1, stride_axis=0)
        full = jnp.where(same, full, 0.0).astype(jnp.bfloat16)
        band_ref[tiles, (count - u) * cols : (count - u + 1) * cols, :] = full


def alive(live_ref, t, slots):
    return jnp.where(t % slots < live_ref[0, t // slots], 1.0, 0.0)


def norms_kernel(width_ref, live_ref, own_ref, other_ref, norm_ref, inv_ref, prow_ref, pcol_ref):
    tiles, size, cols = own_ref.shape
    blocks = size // cols
    lane = lax.broadcasted_iota(jnp.int32, (size, cols), 1)
    keep = (lane >= cols // 2) == (lax.axis_index("band") == 1)
    slots = width_ref.shape[3]
    down = lax.broadcasted_iota(jnp.int32, (cols, cols), 0)
    across = lax.broadcasted_iota(jnp.int32, (cols, cols), 1)
    gaps = (down - across, (down + cols - across)[:8], (down - cols - across)[-8:])
    squares = [(gap * gap).astype(jnp.float32) for gap in gaps]
    spot = lax.broadcasted_iota(jnp.int32, (8, 128), 1)
    spot_low = spot.astype(jnp.float32) - PW

    def table(width):
        width = jnp.full((8, 128), width, jnp.float32)
        rate = -0.5 / (width * width)
        base = jnp.where(spot <= 2 * PW, jnp.exp(spot_low * spot_low * rate), 0.0)
        scale = 1.0 / jnp.sum(base[0:1], axis=1, keepdims=True)
        return [
            jnp.where(square <= float(PW * PW), jnp.exp(square * rate[0:1, 0:1]) * scale, 0.0)
            for square in squares
        ]

    def gap(rows):
        return jnp.zeros((rows, cols), jnp.float32)

    def row_matrix(main, low, high):
        up = jnp.concatenate([gap(cols - 8), high], axis=0)
        under = jnp.concatenate([low, gap(cols - 8)], axis=0)
        choice = {0: main, 1: up, -1: under}
        return jnp.concatenate(
            [
                jnp.concatenate([choice.get(b - a, gap(cols)) for b in range(blocks)], axis=1)
                for a in range(blocks)
            ],
            axis=0,
        ).astype(jnp.bfloat16)

    def column_matrix(main, low, high):
        return jnp.concatenate([main, low, gap(cols - 16), high], axis=0).astype(jnp.bfloat16)

    def one(t, carry):
        inv_own = 1.0 / own_ref[t]
        inv_ref[t] = inv_own
        inv_other = jnp.where(keep, 1.0 / other_ref[t], 0.0)
        inv_low = jnp.concatenate([inv_own, inv_other], axis=1).astype(jnp.bfloat16)
        prow = table(width_ref[0, t // slots, 0, t % slots])
        pcol = table(width_ref[0, t // slots, 1, t % slots])
        prow_ref[t] = row_matrix(*prow)
        pcol_ref[t] = column_matrix(*pcol)
        qrow = row_matrix(*[value * value for value in prow])
        qcol = column_matrix(*[value * value for value in pcol])
        denom = jnp.dot(qrow, inv_low, preferred_element_type=jnp.float32).astype(jnp.bfloat16)
        denom = jnp.dot(denom, qcol, preferred_element_type=jnp.float32)
        norm_ref[t] = alive(live_ref, t, slots) / jnp.sqrt(denom)
        return carry

    lax.fori_loop(0, tiles, one, 0, unroll=tiles)


PAD = 16


def place(ids_ref, t, owned, closed):
    slots = ids_ref.shape[2]
    row = lax.axis_index("exp")
    rows = lax.axis_size("exp")
    columns = lax.axis_size("patch")
    flip = lax.rem(lax.axis_index("groups"), 2) if closed else 0
    name = ids_ref[0, t // slots, t % slots]
    step = name // (owned * columns)
    column = name - step * (owned * columns)
    owner = column // owned
    shift = lax.rem(owner - lax.axis_index("patch") + columns, columns)
    inside = (row + step >= 1) & (row + step <= rows)
    step = jnp.where(flip == 0, step, 2 - step)
    return step * columns + shift, column - owner * owned, jnp.where(inside, 1.0, 0.0)


def clear_ends(padded_ref):
    cols = padded_ref.shape[2]
    for n in range(padded_ref.shape[0]):
        padded_ref[n, 0:PAD, :] = jnp.zeros((PAD, cols), jnp.float32)
        padded_ref[n, -PAD:, :] = jnp.zeros((PAD, cols), jnp.float32)


def build(padded_ref, lhs_ref, n):
    pairs = lhs_ref.shape[1]
    cols = padded_ref.shape[2]
    for r in range(2 * HW + 2):
        lhs_ref[n, :, r * cols : (r + 1) * cols] = padded_ref[
            n, pl.ds(PAD - HW + r, pairs, stride=2), :
        ].astype(jnp.bfloat16)


def spread(lhs_ref, band_ref, n, which):
    cols = band_ref.shape[2]
    count = 2 * HW + 2
    weights = jnp.concatenate(
        [band_ref[which, cols:, :], band_ref[which, : count * cols, :]], axis=1
    )
    return jnp.dot(lhs_ref[n], weights, preferred_element_type=jnp.float32)


def multiply_kernel(members, closed, carried, ids_ref, *refs):
    blocks = refs[: len(members)]
    band_ref = refs[len(members)]
    conv_ref, padded_ref, lhs_ref, list_ref = refs[len(members) + 1 + carried :]
    tiles, size, cols = conv_ref.shape
    owned = blocks[0].shape[0]
    side, pairs = lhs_ref.shape[0] // 2, lhs_ref.shape[1]
    clear_ends(padded_ref)

    count = 0
    for t in range(tiles):
        part, _, _ = place(ids_ref, t, owned, closed)
        here = functools.reduce(lambda a, b: a | b, [part == b for b in members])

        @pl.when(here)
        def _(t=t, count=count):
            list_ref[count] = t

        count = count + jnp.where(here, 1, 0)

    groups = (count + side - 1) // side

    def named_tile(i, n):
        return list_ref[jnp.minimum(i * side + n, count - 1)]

    def pick(i, base):
        for n in range(side):
            part, slot, _ = place(ids_ref, named_tile(i, n), owned, closed)
            for b, ref in zip(members, blocks):
                @pl.when(part == b)
                def _(n=n, ref=ref, slot=slot):
                    padded_ref[base + n, PAD : PAD + size, :] = ref[slot].astype(jnp.float32)

    def work(i, base, following):
        for n in range(side):
            t = named_tile(i, n)
            both = spread(lhs_ref, band_ref, base + n, t)
            build(padded_ref, lhs_ref, following + n)
            for s in range(2):
                conv_ref[t, pl.ds(s, pairs, stride=2), :] = both[:, s * cols : (s + 1) * cols]

    @pl.when(count > 0)
    def _():
        pick(0, 0)
        for n in range(side):
            build(padded_ref, lhs_ref, n)

    def some(i, carry):
        pick(2 * i + 1, side)
        work(2 * i, 0, side)

        @pl.when(2 * i + 1 < groups)
        def _():
            pick(2 * i + 2, 0)
            work(2 * i + 1, side, 0)

        return carry

    lax.fori_loop(0, (groups + 1) // 2, some, 0)


def convolve_kernel(blocks, closed, pieces, ids_ref, live_ref, *refs):
    other_blocks = refs[:blocks]
    (conv_ref, band_ref, exp_ref, inv_ref, low_ref) = refs[blocks : blocks + 5]
    out_refs = refs[blocks + 5 : blocks + 5 + len(pieces)]
    tile_ref, padded_ref, lhs_ref, edge_ref, acc_ref = refs[blocks + 5 + len(pieces) :]
    tiles, size, cols = tile_ref.shape
    owned = other_blocks[0].shape[0]
    slots = ids_ref.shape[2]
    group = cols // tiles
    pairs = size // 2
    core = lax.axis_index("band")

    for t in range(tiles):
        part, slot, _ = place(ids_ref, t, owned, closed)
        for b in range(blocks):
            @pl.when(part == b)
            def _(t=t, b=b, slot=slot):
                tile_ref[t] = other_blocks[b][slot]

    acc_ref[...] = jnp.zeros_like(acc_ref)
    clear_ends(padded_ref)
    lane = lax.broadcasted_iota(jnp.int32, (1, cols), 1)
    start = jnp.where(core == 0, 0, cols - group)
    target = cols - group - start
    strip = jnp.zeros((size, cols), jnp.float32)
    for t in range(tiles):
        moved = pltpu.roll(tile_ref[t].astype(jnp.float32), lax.rem(t * group - start + cols, cols), 1)
        strip = jnp.where(lane // group == t, moved, strip)
    padded_ref[0, PAD : PAD + size, :] = strip
    build(padded_ref, lhs_ref, 0)
    both = spread(lhs_ref, band_ref, 0, tiles)
    for s in range(2):
        edge_ref[pl.ds(s, pairs, stride=2), :] = both[:, s * cols : (s + 1) * cols]

    def one(t, carry):
        edge = pltpu.roll(edge_ref[...], lax.rem(target - t * group + cols, cols), 1)
        edge = jnp.where((lane >= target) & (lane < target + group), edge, 0.0)
        part, slot, present = place(ids_ref, t, owned, closed)
        convolved = (conv_ref[t] + edge) * present
        own = (exp_ref[t].astype(jnp.float32) - convolved) * inv_ref[t]
        low_ref[t] = own.astype(jnp.bfloat16)
        acc_ref[part * owned + slot] += alive(live_ref, t, slots) * own
        return carry

    lax.fori_loop(0, tiles, one, 0, unroll=8)
    for ref, (b, begin, end) in zip(out_refs, pieces):
        ref[...] = acc_ref[b * owned + begin : b * owned + end].astype(ref.dtype)


def score_kernel(low_ref, other_ref, prow_ref, pcol_ref, norm_ref, score_ref):
    tiles, size, cols = low_ref.shape
    lane = lax.broadcasted_iota(jnp.int32, (size, cols), 1)
    keep = (lane >= cols // 2) == (lax.axis_index("band") == 1)

    def one(t, carry):
        other = jnp.where(keep, other_ref[t].astype(jnp.float32), 0.0).astype(jnp.bfloat16)
        full = jnp.concatenate([low_ref[t], other], axis=1)
        numer = jnp.dot(prow_ref[t], full, preferred_element_type=jnp.float32)
        numer = numer.astype(jnp.bfloat16)
        numer = jnp.dot(numer, pcol_ref[t], preferred_element_type=jnp.float32)
        score_ref[t] = numer * norm_ref[t]
        return carry

    lax.fori_loop(0, tiles, one, 0, unroll=tiles)


def merge_kernel(closed, here_ref, first_ref, last_ref, *refs):
    row = lax.axis_index("exp")
    rows = lax.axis_size("exp")
    flip = lax.rem(lax.axis_index("groups"), 2) if closed else 0
    has_first = jnp.where(flip == 0, row > 0, row < rows - 1)
    has_last = jnp.where(flip == 0, row < rows - 1, row > 0)
    out_ref, made_ref, sem = refs[-3:]
    come = refs[:-3]
    owned = here_ref.shape[0]
    cuts = halves(owned)
    moves = []
    for patch in range(owned):
        total = here_ref[patch].astype(jnp.float32)
        total = total + jnp.where(has_first, first_ref[patch].astype(jnp.float32), 0.0)
        total = total + jnp.where(has_last, last_ref[patch].astype(jnp.float32), 0.0)
        for n, ref in enumerate(come):
            begin, end = cuts[n % len(cuts)]
            if begin <= patch < end:
                total = total + ref[patch - begin].astype(jnp.float32)
        if not come:
            out_ref[patch] = total.astype(out_ref.dtype)
        else:
            made_ref[patch] = total
            moves.append(pltpu.make_async_copy(made_ref.at[patch], out_ref.at[patch], sem.at[patch]))
            moves[-1].start()
    for move in moves:
        move.wait()


def halves(count):
    return [(0, count // 2), (count // 2, count)] if count % 2 == 0 else [(0, count)]


def shape(dims, dtype):
    return jax.ShapeDtypeStruct(dims, dtype)


def vmem(count):
    return [pl.BlockSpec(memory_space=VMEM)] * count


def smem(count):
    return [pl.BlockSpec(memory_space=SMEM)] * count


def params(mib):
    return pltpu.CompilerParams(vmem_limit_bytes=mib << 20)


def cost(micros):
    return pl.CostEstimate(flops=int(micros * 1e9), bytes_accessed=int(micros * 3e6), transcendentals=0)


def on_device(templates, exposures, variance, coefficients, psf_width, patch_ids, live_count):
    size = templates.shape[2]
    cols = templates.shape[3]
    owned = templates.shape[1]
    across = lax.axis_size("patch")
    blocks = 3 * across
    low = jnp.bfloat16
    f32 = jnp.float32

    own = templates.reshape(owned, size, cols)
    exp_flat = exposures.reshape(-1, size, cols)
    var_flat = variance.reshape(-1, size, cols)
    tiles = exp_flat.shape[0]
    assert cols % tiles == 0 and cols // tiles >= HW and size % cols == 0 and PW < 8
    swap = functools.partial(sent, axis="band", distance=1)

    forth, back, closed = neighbours(lax.axis_size("groups"), lax.axis_size("exp"))
    ahead = lambda block: lax.ppermute(block, ("groups", "exp"), forth)
    behind = lambda block: lax.ppermute(block, ("groups", "exp"), back)
    row = [own] + [fetched(own, "patch", d) for d in range(1, across)]
    firsts = [ahead(own)]
    lasts = [behind(own)]
    var_other = swap(var_flat)

    count = 2 * HW + 1
    held = -(-count // 8) * 8
    band = pl.pallas_call(
        taps_kernel,
        name="taps",
        out_shape=shape((tiles + 1, (count + 2) * cols, cols), low),
        in_specs=smem(1),
        out_specs=vmem(1)[0],
        scratch_shapes=[VMEM((tiles, held, cols), f32), VMEM((tiles, held, cols), f32)],
        compiler_params=params(4),
        cost_estimate=cost(3),
    )(coefficients)
    band, row = lax.optimization_barrier((band, row))
    firsts += [ahead(row[d]) for d in range(1, across)]
    lasts += [behind(row[d]) for d in range(1, across)]

    norm, inv, prow, pcol = pl.pallas_call(
        norms_kernel,
        name="norms",
        out_shape=(
            shape((tiles, size, cols), f32),
            shape((tiles, size, cols), f32),
            shape((tiles, size, size), low),
            shape((tiles, 2 * cols, cols), low),
        ),
        in_specs=smem(2) + vmem(2),
        out_specs=tuple(vmem(4)),
        compiler_params=params(6),
        cost_estimate=cost(5),
    )(jnp.swapaxes(psf_width, 2, 3), live_count, var_flat, var_other)
    side = 1

    def multiply(members, sources, *carried):
        return pl.pallas_call(
            functools.partial(multiply_kernel, members, closed, len(carried)),
            name="multiply",
            out_shape=shape((tiles, size, cols), f32),
            in_specs=smem(1) + vmem(len(sources) + 1 + len(carried)),
            out_specs=vmem(1)[0],
            input_output_aliases={len(sources) + 2: 0} if carried else {},
            scratch_shapes=[
                VMEM((2 * side, size + 2 * PAD, cols), f32),
                VMEM((2 * side, size // 2, (count + 1) * cols), low),
                SMEM((tiles,), jnp.int32),
            ],
            compiler_params=params(8),
            cost_estimate=cost(3),
        )(patch_ids, *sources, band, *carried)

    soon = [0] + list(range(across, 2 * across)) + [2 * across]
    conv = multiply(soon, [firsts[0]] + row + [lasts[0]])
    norm, conv, firsts[1:], lasts[1:] = lax.optimization_barrier(
        (norm, conv, firsts[1:], lasts[1:])
    )
    early = [swap(b) for b in [firsts[0]] + row + [lasts[0]]]
    later = [b for b in range(blocks) if b not in soon]
    if later:
        conv = multiply(later, firsts[1:] + lasts[1:], conv)
    window_other = early[:1] + [swap(b) for b in firsts[1:]] + early[1:-1]
    window_other = window_other + early[-1:] + [swap(b) for b in lasts[1:]]

    cuts = halves(owned)
    pieces = [(b, 0, owned) for b in (0, across, 2 * across)]
    pieces += [(n * across + d, *cut) for d in range(1, across) for cut in cuts for n in range(3)]
    outs = pl.pallas_call(
        functools.partial(convolve_kernel, blocks, closed, pieces),
        name="convolve",
        out_shape=tuple(
            [shape((tiles, size, cols), low)]
            + [shape((e - a, size, cols), f32 if b == across else low) for b, a, e in pieces]
        ),
        in_specs=smem(2) + vmem(blocks + 4),
        out_specs=tuple(vmem(1 + len(pieces))),
        scratch_shapes=[
            VMEM((tiles, size, cols), low),
            VMEM((1, size + 2 * PAD, cols), f32),
            VMEM((1, size // 2, (count + 1) * cols), low),
            VMEM((size, cols), f32),
            VMEM((blocks * owned, size, cols), f32),
        ],
        compiler_params=params(12),
        cost_estimate=cost(5),
    )(patch_ids, live_count, *window_other, conv, band, exp_flat, inv)
    weighted_low = outs[0]
    parts = dict(zip(pieces, outs[1:]))
    whole = (0, owned)
    weighted_other = swap(weighted_low)
    from_ahead = ahead(parts[(2 * across, *whole)])
    from_behind = behind(parts[(0, *whole)])

    def merge(dtype, here, *arrays):
        final = len(arrays) > 2
        return pl.pallas_call(
            functools.partial(merge_kernel, closed),
            name="merge",
            out_shape=shape(here.shape, dtype),
            in_specs=vmem(1 + len(arrays)),
            out_specs=pl.BlockSpec(memory_space=pl.ANY if final else VMEM),
            scratch_shapes=[
                VMEM(here.shape if final else (1, 8, 128), f32),
                pltpu.SemaphoreType.DMA((here.shape[0],)),
            ],
            compiler_params=params(4),
            cost_estimate=cost(0.5),
        )(here, *arrays)

    come = []
    for d in range(1, across):
        for cut in cuts:
            merged = merge(
                low,
                parts[(across + d, *cut)],
                ahead(parts[(2 * across + d, *cut)]),
                behind(parts[(d, *cut)]),
            )
            come.append(sent(merged, "patch", d))
    score = pl.pallas_call(
        score_kernel,
        name="score",
        out_shape=shape((tiles, size, cols), f32),
        in_specs=vmem(5),
        out_specs=vmem(1)[0],
        compiler_params=params(4),
        cost_estimate=cost(5),
    )(weighted_low, weighted_other, prow, pcol, norm)

    score, come = lax.optimization_barrier((score, come))
    total = merge(f32, parts[(across, *whole)], from_ahead, from_behind, *come)
    return (total.reshape(1, owned, size, cols), score.reshape(exposures.shape))


def solution(mesh):
    assert mesh.shape["band"] == 2
    in_specs = (
        P(("groups", "exp"), "patch", None, "band"),
        P(("groups", "exp"), "patch", None, None, "band"),
        P(("groups", "exp"), "patch", None, None, "band"),
        P(("groups", "exp"), "patch", None, None),
        P(("groups", "exp"), "patch", None, None),
        P(("groups", "exp"), "patch", None),
        P(("groups", "exp"), "patch"),
    )
    out_specs = (
        P(("groups", "exp"), "patch", None, "band"),
        P(("groups", "exp"), "patch", None, None, "band"),
    )

    def step(*args):
        return on_device(*args)

    step = jax.shard_map(step, mesh=mesh, in_specs=in_specs, out_specs=out_specs, check_vma=False)
    return step
```
